32 devices in a mesh: groups: 2 (over x), lon: 16 (over z, y, core).
Axes of the slice: x: 2, y: 2, z: 4, core: 2. Of those that a mesh axis runs over, the one named last changes fastest.
Arguments:
- input_field: bfloat16 [96, 512, 512], P('groups', 'lon'), parts along dimension 0, may hold values from -8 to 8
- expand_weight: bfloat16 [512, 2048], replicated, may hold values from -0.25 to 0.25
- expand_bias: float32 [2048], replicated, may hold values from -3 to 3
- depth_weight: float32 [9, 2048], replicated, may hold values from -2 to 2
- depth_bias: float32 [2048], replicated, may hold values from -3 to 3
- squeeze_down: bfloat16 [2048, 128], replicated, may hold values from -0.125 to 0.125
- squeeze_up: bfloat16 [128, 2048], replicated, may hold values from -3 to 3
- project_weight: bfloat16 [2048, 512], replicated, may hold values from -0.125 to 0.125
- block_gain: float32 [512], replicated, may hold values from 0.1 to 1.9
- block_in_weight: bfloat16 [512, 1536], replicated, may hold values from -4 to 4
- block_out_weight: bfloat16 [512, 512], replicated, may hold values from -0.25 to 0.25
- block_table: float32 [225, 16], replicated, may hold values from -5 to 5
- grid_gain: float32 [512], replicated, may hold values from 0.1 to 1.9
- grid_in_weight: bfloat16 [512, 1536], replicated, may hold values from -4 to 4
- grid_out_weight: bfloat16 [512, 512], replicated, may hold values from -0.25 to 0.25
- grid_table: float32 [225, 16], replicated, may hold values from -5 to 5
Outputs:
- output_field: bfloat16 [96, 512, 512], P('groups', 'lon'), parts along dimension 0
The draws below stay inside these ranges and needn't reach their ends.
There are 2 independent parts, one for each index of `groups`. The reference program is written for one: setup_inputs(seed, part) draws one part's arguments, and reference() takes and returns one part's arrays. A program takes and returns all parts, laid end to end along the dimension named above; an argument that names none is the same for every part. Nothing has to cross between parts.
All inputs are finite; a program needn't handle non-finite values.
Results may differ from the reference program's by a relative error of at most 0.012.
Values may be sent and summed in bfloat16 or wider, within the bound.
No kernel may reach another device: no remote copies, remote signals or barrier semaphores. Data moves between devices by JAX's collectives and lax.ppermute only.
A program may use at most 128 MiB of HBM per device.

```python
import jax
import jax.numpy as jnp
from jax import lax

CHANNELS = 512
HEADS = 16
SQUEEZE = 128
HEAD_DIM = 32
EXPANDED = 2048
ROWS = 48
WIDTH = 512


def draw_input_field(key, part):
    key_one = jax.random.fold_in(key, 0)
    position = jnp.arange(WIDTH, dtype=jnp.float32) / WIDTH
    basic_draw = jax.random.normal(key_one, (ROWS, WIDTH, CHANNELS), jnp.float32)
    values = basic_draw * (0.5 + position)[None, :, None]
    return jnp.clip(values, -8.0, 8.0).astype(jnp.bfloat16)


def drawn_projection(key, salt):
    key_one = jax.random.fold_in(key, salt)
    spread_scale = CHANNELS ** (-0.5)
    basic_draw = jax.random.normal(key_one, (CHANNELS, 3 * CHANNELS), jnp.float32) * spread_scale
    return jnp.clip(basic_draw, -4.0, 4.0)


def draw_block_in_weight(key, part):
    return drawn_projection(key, 11).astype(jnp.bfloat16)


def draw_grid_in_weight(key, part):
    return drawn_projection(key, 23).astype(jnp.bfloat16)


def normal_values(stream_key, extent, width, limit, held_as=jnp.bfloat16):
    return jnp.clip(width * jax.random.normal(stream_key, extent, jnp.float32), -limit, limit).astype(held_as)


def setup_inputs(seed: int = 0, part: int = 0) -> dict:
    key_list = jax.random.split(jax.random.key(seed), 17)
    part_splits = jax.random.split(jax.random.fold_in(key_list[16], part), 17)
    return {
        "input_field": draw_input_field(jax.random.fold_in(jax.random.fold_in(key_list[16], part), 71), part),
        "expand_weight": normal_values(key_list[1], (CHANNELS, EXPANDED), CHANNELS ** -0.5, 0.25),
        "expand_bias": normal_values(key_list[2], (EXPANDED,), 0.5, 3.0, jnp.float32),
        "depth_weight": normal_values(key_list[3], (9, EXPANDED), 9 ** -0.5, 2.0, jnp.float32),
        "depth_bias": normal_values(key_list[4], (EXPANDED,), 0.5, 3.0, jnp.float32),
        "squeeze_down": normal_values(key_list[5], (EXPANDED, SQUEEZE), EXPANDED ** -0.5, 0.125),
        "squeeze_up": normal_values(key_list[6], (SQUEEZE, EXPANDED), 0.5, 3.0),
        "project_weight": normal_values(key_list[7], (EXPANDED, CHANNELS), EXPANDED ** -0.5, 0.125),
        "block_gain": jnp.clip(1.0 + 0.18 * jax.random.normal(key_list[8], (CHANNELS,), jnp.float32), 0.1, 1.9),
        "block_in_weight": draw_block_in_weight(jax.random.fold_in(key_list[16], 71), part),
        "block_out_weight": normal_values(key_list[10], (CHANNELS, CHANNELS), CHANNELS ** -0.5, 0.25),
        "block_table": normal_values(key_list[11], (225, HEADS), 1.0, 5.0, jnp.float32),
        "grid_gain": jnp.clip(1.0 + 0.18 * jax.random.normal(key_list[12], (CHANNELS,), jnp.float32), 0.1, 1.9),
        "grid_in_weight": draw_grid_in_weight(jax.random.fold_in(key_list[16], 71), part),
        "grid_out_weight": normal_values(key_list[14], (CHANNELS, CHANNELS), CHANNELS ** -0.5, 0.25),
        "grid_table": normal_values(key_list[15], (225, HEADS), 1.0, 5.0, jnp.float32),
    }


def relative_bias(pos_table):
    position = jnp.arange(64)
    win_row = position // 8
    win_col = position % 8
    rel_index = (win_row[:, None] - win_row[None, :] + 7) * 15 + (win_col[:, None] - win_col[None, :] + 7)
    one_hot = (rel_index[:, :, None] == jnp.arange(225)[None, None, :]).astype(jnp.float32)
    return jnp.einsum('ijr,rh->hij', one_hot, pos_table, precision=lax.Precision.HIGHEST)

def window_attention(tokens, gain, in_weight, out_weight, rel_bias):
    win_count = tokens.shape[0]
    channels = tokens.shape[-1]
    widened = tokens.astype(jnp.float32)
    average = lax.optimization_barrier(jnp.mean(widened, axis=-1, keepdims=True))
    centred = widened - average
    variance = lax.optimization_barrier(jnp.mean(centred * centred, axis=-1, keepdims=True))
    normed = (centred * lax.rsqrt(variance + 1e-05) * gain).astype(jnp.bfloat16)
    mixed = jnp.dot(normed.reshape(-1, channels), in_weight, preferred_element_type=jnp.float32).astype(jnp.bfloat16)
    mixed = mixed.reshape(win_count, 64, 3, HEADS, HEAD_DIM).astype(jnp.float32)
    scores = jnp.einsum('nqhd,nkhd->nhqk', mixed[:, :, 0], mixed[:, :, 1], precision=lax.Precision.HIGHEST)
    scores = scores * HEAD_DIM ** (-0.5) + rel_bias[None]
    scores = scores - lax.optimization_barrier(jnp.max(scores, axis=-1, keepdims=True))
    exponent = jnp.exp(scores)
    probabilities = (exponent / lax.optimization_barrier(jnp.sum(exponent, axis=-1, keepdims=True))).astype(jnp.bfloat16)
    heads_out = jnp.einsum('nhqk,nkhd->nqhd', probabilities.astype(jnp.float32), mixed[:, :, 2], precision=lax.Precision.HIGHEST).astype(jnp.bfloat16)
    merged = jnp.dot(heads_out.reshape(-1, channels), out_weight, preferred_element_type=jnp.float32)
    return (widened.reshape(-1, channels) + merged).astype(jnp.bfloat16).reshape(win_count, 64, channels)

def attend_all(windows, gain, in_weight, out_weight, pos_table):
    rel_bias = relative_bias(pos_table)
    channels = windows.shape[-1]
    batches = windows.reshape(8, -1, 64, channels)

    def one_batch(subset):
        return window_attention(subset, gain, in_weight, out_weight, rel_bias)
    result = lax.map(one_batch, batches)
    return result.reshape(-1, 64, channels)

def mbconv_block(input_field, expand_weight, expand_bias, depth_weight, depth_bias, squeeze_down, squeeze_up, project_weight):
    row_count, col_count, channels = input_field.shape
    hidden = jnp.dot(input_field.reshape(-1, channels), expand_weight, preferred_element_type=jnp.float32) + expand_bias
    hidden = jax.nn.gelu(hidden, approximate=False).astype(jnp.bfloat16).reshape(row_count, col_count, -1)
    padded = jnp.concatenate([hidden[:, -1:], hidden, hidden[:, :1]], axis=1)
    padded = jnp.pad(padded, ((1, 1), (0, 0), (0, 0)))
    summed = depth_bias + jnp.zeros((row_count, col_count, depth_bias.shape[0]), jnp.float32)
    for row_off in range(3):
        for col_off in range(3):
            summed = summed + padded[row_off:row_off + row_count, col_off:col_off + col_count].astype(jnp.float32) * depth_weight[row_off * 3 + col_off]
    active = jax.nn.gelu(summed, approximate=False).astype(jnp.bfloat16)
    pooled = lax.optimization_barrier(jnp.sum(active.astype(jnp.float32), axis=(0, 1))) / (row_count * col_count)
    squeezed = jax.nn.silu(jnp.dot(pooled, squeeze_down.astype(jnp.float32), precision=lax.Precision.HIGHEST))
    gate_value = jax.nn.sigmoid(jnp.dot(squeezed, squeeze_up.astype(jnp.float32), precision=lax.Precision.HIGHEST))
    gated_act = (active.astype(jnp.float32) * gate_value).astype(jnp.bfloat16)
    result = jnp.dot(gated_act.reshape(-1, gated_act.shape[-1]), project_weight, preferred_element_type=jnp.float32)
    result = result + input_field.reshape(-1, channels).astype(jnp.float32)
    return result.astype(jnp.bfloat16).reshape(row_count, col_count, channels)

def reference(input_field, expand_weight, expand_bias, depth_weight, depth_bias, squeeze_down, squeeze_up, project_weight, block_gain, block_in_weight, block_out_weight, block_table, grid_gain, grid_in_weight, grid_out_weight, grid_table):
    first_stream = mbconv_block(input_field, expand_weight, expand_bias, depth_weight, depth_bias, squeeze_down, squeeze_up, project_weight)
    row_count, col_count, channels = first_stream.shape
    blocks = first_stream.reshape(row_count // 8, 8, col_count // 8, 8, channels).transpose(0, 2, 1, 3, 4).reshape(-1, 64, channels)
    blocks = attend_all(blocks, block_gain, block_in_weight, block_out_weight, block_table)
    second_stream = blocks.reshape(row_count // 8, col_count // 8, 8, 8, channels).transpose(0, 2, 1, 3, 4).reshape(row_count, col_count, channels)
    cells = second_stream.reshape(8, row_count // 8, 8, col_count // 8, channels).transpose(1, 3, 0, 2, 4).reshape(-1, 64, channels)
    cells = attend_all(cells, grid_gain, grid_in_weight, grid_out_weight, grid_table)
    return cells.reshape(row_count // 8, col_count // 8, 8, 8, channels).transpose(2, 0, 3, 1, 4).reshape(row_count, col_count, channels)
```

```python
import functools

import jax
import jax.numpy as jnp
import numpy as np
from jax import lax
from jax.experimental import pallas as pl
from jax.experimental.pallas import tpu as pltpu
from jax.sharding import PartitionSpec as P

HEADS = 16
HEAD_DIM = 32
WIN = 8
CELLS = WIN * WIN
CHUNKS = (2, 2)
LANES = 256
LOG2E = 1.4426950408889634
SCORE_SCALE = HEAD_DIM ** (-0.5) * LOG2E
BF16 = jnp.bfloat16
F32 = jnp.float32


def gelu(value):
    return 0.5 * value * (1.0 + lax.erf(value * 0.7071067811865476))


def mbconv_kernel(x_ref, w_ref, b_ref, dw_ref, db_ref, down_ref, act_ref, part_ref, hid_ref):
    cols, rows, channels = x_ref.shape
    lanes = w_ref.shape[1]
    step = 2
    bias = b_ref[...]

    def expand(i, carry):
        cells = x_ref[pl.ds(i * step, step)].reshape(step * rows, channels)
        hidden = jnp.dot(cells, w_ref[...], preferred_element_type=F32) + bias
        hid_ref[pl.ds(i * step, step)] = gelu(hidden).reshape(step, rows, lanes)
        return carry

    lax.fori_loop(0, cols // step, expand, 0)
    row = lax.broadcasted_iota(jnp.int32, (rows, lanes), 0)
    first = row == 0
    last = row == rows - 1
    taps = dw_ref[...]
    shift = db_ref[...]

    def depth(c, total):
        sums = []
        for r in range(3):
            acc = hid_ref[c] * taps[3 * r : 3 * r + 1]
            acc = acc + hid_ref[c + 1] * taps[3 * r + 1 : 3 * r + 2]
            acc = acc + hid_ref[c + 2] * taps[3 * r + 2 : 3 * r + 3]
            sums.append(acc)
        above = jnp.where(first, 0.0, pltpu.roll(sums[0], 1, 0))
        below = jnp.where(last, 0.0, pltpu.roll(sums[2], rows - 1, 0))
        active = gelu(sums[1] + above + (below + shift))
        act_ref[c] = active.astype(BF16)
        return total + active.reshape(rows // 8, 8, lanes).sum(0)

    total = lax.fori_loop(0, cols - 2, depth, jnp.zeros((8, lanes), F32))
    pooled = jnp.sum(total, axis=0, keepdims=True)
    part = jnp.dot(
        jnp.broadcast_to(pooled, (8, lanes)),
        down_ref[...].astype(F32),
        precision=lax.Precision.HIGHEST,
        preferred_element_type=F32,
    )

    @pl.when(pl.program_id(0) == 0)
    def _():
        part_ref[...] = part

    @pl.when(pl.program_id(0) > 0)
    def _():
        part_ref[...] += part


def mbconv(rimmed, expand_weight, expand_bias, depth_weight, depth_bias, squeeze_down):
    cols, rows, channels = rimmed.shape
    expanded = expand_weight.shape[1]
    squeeze = squeeze_down.shape[1]
    return pl.pallas_call(
        mbconv_kernel,
        name="mbconv",
        grid=(expanded // LANES,),
        in_specs=[
            pl.BlockSpec((cols, rows, channels), lambda i: (0, 0, 0), pipeline_mode=pl.Buffered(1)),
            pl.BlockSpec((channels, LANES), lambda i: (0, i)),
            pl.BlockSpec((1, LANES), lambda i: (0, i)),
            pl.BlockSpec((9, LANES), lambda i: (0, i)),
            pl.BlockSpec((1, LANES), lambda i: (0, i)),
            pl.BlockSpec((LANES, squeeze), lambda i: (i, 0)),
        ],
        out_specs=[
            pl.BlockSpec((cols - 2, rows, LANES), lambda i: (0, 0, i)),
            pl.BlockSpec((8, squeeze), lambda i: (0, 0)),
        ],
        out_shape=[
            jax.ShapeDtypeStruct((cols - 2, rows, expanded), BF16),
            jax.ShapeDtypeStruct((8, squeeze), F32),
        ],
        scratch_shapes=[pltpu.VMEM((cols, rows, LANES), F32)],
        cost_estimate=pl.CostEstimate(
            flops=2 * cols * rows * channels * expanded * 4,
            bytes_accessed=20_000_000,
            transcendentals=0,
        ),
        compiler_params=pltpu.CompilerParams(vmem_limit_bytes=32 << 20),
    )(
        rimmed,
        expand_weight,
        expand_bias.reshape(1, -1),
        depth_weight,
        depth_bias.reshape(1, -1),
        squeeze_down,
    )


def attend(stream, gain_ref, wq_ref, wk_ref, wv_ref, wo_ref, bias_ref, mask_ref, scratch):
    q_ref, k_ref, vt_ref, o_ref = scratch
    cells, channels = stream.shape
    average = jnp.mean(stream, axis=-1, keepdims=True)
    centred = stream - average
    variance = jnp.mean(centred * centred, axis=-1, keepdims=True)
    normed = (centred * lax.rsqrt(variance + 1e-05) * gain_ref[...]).astype(BF16)
    q_ref[...] = jnp.dot(normed, wq_ref[...], preferred_element_type=F32).astype(BF16)
    k_ref[...] = jnp.dot(normed, wk_ref[...], preferred_element_type=F32).astype(BF16)
    vt_ref[...] = lax.dot_general(
        wv_ref[...], normed, (((1,), (1,)), ((), ())), preferred_element_type=F32
    ).astype(BF16)
    mask = mask_ref[...]
    group = 256 // HEAD_DIM
    even = (lax.broadcasted_iota(jnp.int32, (CELLS, 128), 1) // HEAD_DIM) % 2 == 0
    for w in range(cells // CELLS):
        span = slice(w * CELLS, (w + 1) * CELLS)
        for g in range(HEADS // group):
            part = slice(g * 256, (g + 1) * 256)
            query = jnp.concatenate([q_ref[span, part]] * group, axis=0) * mask
            lanes = slice(g * group * CELLS, (g + 1) * group * CELLS)
            scores = lax.dot_general(
                k_ref[span, part], query, (((1,), (1,)), ((), ())), preferred_element_type=F32
            )
            scores = scores * SCORE_SCALE + bias_ref[:, lanes]
            scores = jnp.exp2(scores - jnp.max(scores, axis=0, keepdims=True))
            weight = 1.0 / jnp.sum(scores, axis=0, keepdims=True)
            prob = (scores * weight).astype(BF16)
            for quad in range(group // 4):
                halves = []
                for pair in (2 * quad, 2 * quad + 1):
                    values = vt_ref[g * 256 + pair * 64 : g * 256 + pair * 64 + 64, span]
                    halves.append(
                        jnp.dot(
                            values,
                            prob[:, pair * 128 : pair * 128 + 128],
                            preferred_element_type=F32,
                        )
                    )
                turned = jnp.concatenate(halves, axis=0).T
                picked = jnp.where(even, turned[:CELLS], turned[CELLS:])
                o_ref[span, g * 256 + quad * 128 : g * 256 + quad * 128 + 128] = picked.astype(BF16)
    return stream + jnp.dot(o_ref[...], wo_ref[...], preferred_element_type=F32)


def block_kernel(
    act_ref, x_ref, part_ref, up_ref, proj_ref, gain_ref, wq_ref, wk_ref, wv_ref, wo_ref,
    bias_ref, mask_ref, out_ref, gate_ref, *scratch,
):
    cols, rows, expanded = act_ref.shape
    channels = x_ref.shape[2]

    @pl.when(pl.program_id(0) == 0)
    def _():
        squeezed = jnp.broadcast_to(part_ref[...], (8, part_ref.shape[1]))
        squeezed = squeezed * jax.nn.sigmoid(squeezed)
        gate = jnp.dot(
            squeezed,
            up_ref[...].astype(F32),
            precision=lax.Precision.HIGHEST,
            preferred_element_type=F32,
        )
        gate_ref[...] = jax.nn.sigmoid(gate)

    gated = act_ref[...].reshape(cols * rows, expanded).astype(F32) * gate_ref[0:1]
    first = jnp.dot(gated.astype(BF16), proj_ref[...], preferred_element_type=F32)
    first = first.reshape(cols, rows, channels) + x_ref[...].astype(F32)
    first = first.astype(BF16).astype(F32)
    windows = rows // WIN
    stream = jnp.concatenate(
        [first[:, a * WIN : (a + 1) * WIN].reshape(CELLS, channels) for a in range(windows)],
        axis=0,
    )
    second = attend(
        stream, gain_ref, wq_ref, wk_ref, wv_ref, wo_ref, bias_ref, mask_ref, scratch
    ).reshape(windows, cols, WIN, channels)
    second = jnp.concatenate([second[a] for a in range(windows)], axis=1)
    out_ref[...] = second.reshape(out_ref.shape).astype(BF16)


def grid_kernel(
    s_ref, perm_ref, back_ref, gain_ref, wq_ref, wk_ref, wv_ref, wo_ref,
    bias_ref, mask_ref, out_ref, *scratch,
):
    cells = perm_ref.shape[0]
    channels = s_ref.shape[-1]
    incoming = s_ref[...].reshape(cells, channels)
    stream = jnp.dot(perm_ref[...], incoming, preferred_element_type=F32)
    result = attend(
        stream, gain_ref, wq_ref, wk_ref, wv_ref, wo_ref, bias_ref, mask_ref, scratch
    ).astype(BF16)
    result = jnp.dot(back_ref[...], result, preferred_element_type=F32)
    out_ref[...] = result.astype(BF16).reshape(out_ref.shape)


def whole(shape):
    return pl.BlockSpec(shape, lambda *_: (0,) * len(shape), pipeline_mode=pl.Buffered(1))


def attention_scratch(cells, channels):
    return [
        pltpu.VMEM((cells, channels), BF16),
        pltpu.VMEM((cells, channels), BF16),
        pltpu.VMEM((channels, cells), BF16),
        pltpu.VMEM((cells, channels), BF16),
    ]


def block_stage(start, count, active, field, part, up, proj, params):
    cols, rows, channels = field.shape
    expanded = active.shape[2]
    cells = WIN * rows
    return pl.pallas_call(
        block_kernel,
        name="block_stage",
        grid=(count,),
        in_specs=[
            pl.BlockSpec((WIN, rows, expanded), lambda b: (b + start, 0, 0)),
            pl.BlockSpec((WIN, rows, channels), lambda b: (b + start, 0, 0)),
        ]
        + [whole(p.shape) for p in (part, up, proj, *params)],
        out_specs=pl.BlockSpec((WIN, 1, rows, channels), lambda b: (0, b, 0, 0)),
        out_shape=jax.ShapeDtypeStruct((WIN, count, rows, channels), BF16),
        scratch_shapes=[pltpu.VMEM((8, expanded), F32)] + attention_scratch(cells, channels),
        cost_estimate=pl.CostEstimate(
            flops=2 * count * cells * channels * (expanded + 4 * channels) * 4,
            bytes_accessed=8_000_000,
            transcendentals=0,
        ),
        compiler_params=pltpu.CompilerParams(vmem_limit_bytes=32 << 20),
    )(active, field, part, up, proj, *params)


def grid_stage(received, perm, back, params):
    _, count, rows, channels = received.shape
    cells = WIN * rows
    spec = pl.BlockSpec((WIN, 1, rows, channels), lambda b: (0, b, 0, 0))
    return pl.pallas_call(
        grid_kernel,
        name="grid_stage",
        grid=(count,),
        in_specs=[spec] + [whole(p.shape) for p in (perm, back, *params)],
        out_specs=spec,
        out_shape=jax.ShapeDtypeStruct(received.shape, BF16),
        scratch_shapes=attention_scratch(cells, channels),
        cost_estimate=pl.CostEstimate(
            flops=2 * count * cells * channels * 4 * channels * 4,
            bytes_accessed=6_000_000,
            transcendentals=0,
        ),
        compiler_params=pltpu.CompilerParams(vmem_limit_bytes=32 << 20),
    )(received, perm, back, *params)


def turned_bias(pos_table):
    position = jnp.arange(CELLS)
    row = position % WIN
    col = position // WIN
    index = (row[None, :] - row[:, None] + 7) * 15 + (col[None, :] - col[:, None] + 7)
    one_hot = (index[:, :, None] == jnp.arange(225)[None, None, :]).astype(F32)
    bias = jnp.einsum("jir,rh->jhi", one_hot, pos_table * LOG2E, precision=lax.Precision.HIGHEST)
    return bias.reshape(CELLS, HEADS * CELLS)


def attention_params(gain, in_weight, out_weight, pos_table, mask):
    channels = gain.shape[0]
    return (
        gain.reshape(1, -1),
        in_weight[:, :channels],
        in_weight[:, channels : 2 * channels],
        in_weight[:, 2 * channels :].T,
        out_weight,
        turned_bias(pos_table),
        mask,
    )


def head_mask():
    group = 256 // HEAD_DIM
    head = np.arange(group * CELLS) // CELLS
    lane = np.arange(256) // HEAD_DIM
    return jnp.asarray(head[:, None] == lane[None, :], BF16)


def grid_order(rows):
    per = rows // WIN
    source = np.zeros(WIN * rows, np.int64)
    for a in range(per):
        for j in range(WIN):
            for i in range(WIN):
                source[(a * WIN + j) * WIN + i] = j * rows + i * per + a
    one_hot = source[:, None] == np.arange(WIN * rows)[None, :]
    return jnp.asarray(one_hot, BF16), jnp.asarray(one_hot.T, BF16)


def per_device(
    input_field,
    expand_weight,
    expand_bias,
    depth_weight,
    depth_bias,
    squeeze_down,
    squeeze_up,
    project_weight,
    block_gain,
    block_in_weight,
    block_out_weight,
    block_table,
    grid_gain,
    grid_in_weight,
    grid_out_weight,
    grid_table,
):
    rows, cols, channels = input_field.shape
    count = lax.axis_size("lon")
    per = count // WIN
    groups = [[j * per + r for j in range(WIN)] for r in range(per)]
    field = jnp.swapaxes(input_field, 0, 1)
    before = lax.ppermute(field[-1:], "lon", [(i, (i + 1) % count) for i in range(count)])
    after = lax.ppermute(field[:1], "lon", [((i + 1) % count, i) for i in range(count)])
    rimmed = jnp.concatenate([before, field, after], axis=0)
    active, part = mbconv(
        rimmed, expand_weight, expand_bias, depth_weight, depth_bias, squeeze_down
    )
    parts = lax.all_to_all(
        jnp.broadcast_to(part[None, :1], (count, 1, part.shape[1])), "lon", 0, 0, tiled=True
    )
    part = jnp.sum(parts, axis=0) / (rows * cols * count)
    mask = head_mask()
    perm, back = grid_order(rows)
    block_params = attention_params(
        block_gain, block_in_weight, block_out_weight, block_table, mask
    )
    grid_params = attention_params(grid_gain, grid_in_weight, grid_out_weight, grid_table, mask)
    exchange = functools.partial(
        lax.all_to_all,
        axis_name="lon",
        split_axis=0,
        concat_axis=0,
        axis_index_groups=groups,
        tiled=True,
    )
    results = []
    start = 0
    total = cols // WIN
    for size in CHUNKS if sum(CHUNKS) == total else (total,):
        sent = block_stage(
            start, size, active, field, part, squeeze_up, project_weight, block_params
        )
        start += size
        result = grid_stage(exchange(sent), perm, back, grid_params)
        results.append(exchange(result))
    merged = jnp.concatenate(results, axis=1)
    return merged.transpose(2, 1, 0, 3).reshape(rows, cols, channels)


def solution(mesh):
    return jax.shard_map(
        per_device,
        mesh=mesh,
        in_specs=(P("groups", "lon", None),) + (P(),) * 15,
        out_specs=P("groups", "lon", None),
        check_vma=False,
    )
```

```python
import functools

import jax
import jax.numpy as jnp
import numpy as np
from jax import lax
from jax.experimental import pallas as pl
from jax.experimental.pallas import tpu as pltpu
from jax.sharding import PartitionSpec as P

HEADS = 16
HEAD_DIM = 32
WIN = 8
CELLS = WIN * WIN
CHUNKS = (1, 3)
LANES = 512
SUB = 256
VMEM_BYTES = 60 << 20
ROOT_HALF = 0.7071067811865476
LOG2E = 1.4426950408889634
SCORE_SCALE = HEAD_DIM ** (-0.5) * LOG2E
BF16 = jnp.bfloat16
F32 = jnp.float32


def double_gelu(half):
    return half + half * lax.erf(half)


def mbconv_kernel(
    x_ref, w_ref, b_ref, dw_ref, db_ref, down_ref, shift_ref, act_ref, part_ref,
    total_ref, tap_ref, *hidden_refs,
):
    cols, rows, channels = x_ref.shape
    lanes = w_ref.shape[1]
    sub = hidden_refs[0].shape[2]
    out_cols = cols - 2
    pieces = 2 if cols % 2 == 0 else 1
    piece = cols // pieces
    shift = shift_ref[...]
    for k in range(9):
        tap_ref[k] = jnp.broadcast_to(dw_ref[k : k + 1] * 0.5, (16, lanes)).astype(BF16)

    def expand(s, i):
        span = slice(s * sub, (s + 1) * sub)
        cells = x_ref[i * piece : (i + 1) * piece].reshape(piece * rows, channels)
        hidden = jnp.dot(cells, w_ref[:, span], preferred_element_type=F32)
        hidden = double_gelu(hidden * ROOT_HALF + b_ref[:, span] * ROOT_HALF)
        hidden_refs[s][i * piece : (i + 1) * piece] = hidden.astype(BF16).reshape(piece, rows, sub)

    def depth(s, c, total):
        span = slice(s * sub, (s + 1) * sub)
        near = [hidden_refs[s][c + k].reshape(rows // 16, 16, sub) for k in range(3)]
        sums = []
        for r in range(3):
            terms = [near[k] * tap_ref[3 * r + k, :, span][None] for k in range(3)]
            sums.append((terms[0] + terms[1] + terms[2]).reshape(rows, sub))
        summed = jnp.dot(shift, jnp.concatenate(sums, axis=0), preferred_element_type=F32)
        active = double_gelu(summed + db_ref[:, span] * ROOT_HALF)
        act_ref[c, :, span] = active.astype(BF16)
        return total + active.reshape(rows // 8, 8, sub).sum(0)

    for i in range(pieces):
        expand(0, i)
    for s in range(len(hidden_refs)):
        total = jnp.zeros((8, sub), F32)
        for i in range(pieces):
            if s + 1 < len(hidden_refs):
                expand(s + 1, i)
            for c in range(i * out_cols // pieces, (i + 1) * out_cols // pieces):
                total = depth(s, c, total)
        total_ref[:, s * sub : (s + 1) * sub] = total
    pooled = jnp.sum(total_ref[...], axis=0, keepdims=True)
    part = jnp.dot(
        jnp.broadcast_to(pooled, (8, lanes)),
        down_ref[...].astype(F32),
        precision=lax.Precision.HIGHEST,
        preferred_element_type=F32,
    )

    @pl.when(pl.program_id(0) == 0)
    def _():
        part_ref[...] = part

    @pl.when(pl.program_id(0) > 0)
    def _():
        part_ref[...] += part


def row_shifts(rows):
    shift = np.zeros((rows, 3 * rows), np.float32)
    for offset in range(3):
        for row in range(rows):
            if 0 <= row + offset - 1 < rows:
                shift[row, offset * rows + row + offset - 1] = 1.0
    return jnp.asarray(shift, BF16)


def mbconv(rimmed, expand_weight, expand_bias, depth_weight, depth_bias, squeeze_down):
    cols, rows, channels = rimmed.shape
    expanded = expand_weight.shape[1]
    squeeze = squeeze_down.shape[1]
    return pl.pallas_call(
        mbconv_kernel,
        name="mbconv",
        grid=(expanded // LANES,),
        in_specs=[
            pl.BlockSpec((cols, rows, channels), lambda i: (0, 0, 0), pipeline_mode=pl.Buffered(1)),
            pl.BlockSpec((channels, LANES), lambda i: (0, i)),
            pl.BlockSpec((1, LANES), lambda i: (0, i)),
            pl.BlockSpec((9, LANES), lambda i: (0, i)),
            pl.BlockSpec((1, LANES), lambda i: (0, i)),
            pl.BlockSpec((LANES, squeeze), lambda i: (i, 0)),
            pl.BlockSpec((rows, 3 * rows), lambda i: (0, 0)),
        ],
        out_specs=[
            pl.BlockSpec((cols - 2, rows, LANES), lambda i: (0, 0, i)),
            pl.BlockSpec((8, squeeze), lambda i: (0, 0)),
        ],
        out_shape=[
            jax.ShapeDtypeStruct((cols - 2, rows, expanded), BF16),
            jax.ShapeDtypeStruct((8, squeeze), F32),
        ],
        scratch_shapes=[pltpu.VMEM((8, LANES), F32), pltpu.VMEM((9, 16, LANES), BF16)]
        + [pltpu.VMEM((cols, rows, SUB), BF16)] * (LANES // SUB),
        cost_estimate=pl.CostEstimate(
            flops=2 * cols * rows * channels * expanded * 4,
            bytes_accessed=20_000_000,
            transcendentals=0,
        ),
        compiler_params=pltpu.CompilerParams(vmem_limit_bytes=VMEM_BYTES),
    )(
        rimmed,
        expand_weight,
        expand_bias.reshape(1, -1),
        depth_weight,
        depth_bias.reshape(1, -1),
        squeeze_down,
        row_shifts(rows),
    )


def prepare(in_ref, wv_ref, mask_ref):
    channels = in_ref.shape[0]
    wv_ref[...] = in_ref[:, 2 * channels :].T
    head = lax.broadcasted_iota(jnp.int32, mask_ref.shape, 0) // CELLS
    lane = lax.broadcasted_iota(jnp.int32, mask_ref.shape, 1) // HEAD_DIM
    mask_ref[...] = (head == lane).astype(F32).astype(BF16)


def attend(stream, gain_ref, in_ref, out_weight_ref, bias_ref, scratch):
    wv_ref, mask_ref, q_ref, k_ref, vt_ref, o_ref = scratch
    cells, channels = stream.shape
    average = jnp.mean(stream, axis=-1, keepdims=True)
    centred = stream - average
    variance = jnp.mean(centred * centred, axis=-1, keepdims=True)
    normed = (centred * lax.rsqrt(variance + 1e-05) * gain_ref[...]).astype(BF16)
    q_ref[...] = jnp.dot(normed, in_ref[:, :channels], preferred_element_type=F32).astype(BF16)
    k_ref[...] = jnp.dot(
        normed, in_ref[:, channels : 2 * channels], preferred_element_type=F32
    ).astype(BF16)
    vt_ref[...] = lax.dot_general(
        wv_ref[...], normed, (((1,), (1,)), ((), ())), preferred_element_type=F32
    ).astype(BF16)
    group = 256 // HEAD_DIM
    even = (lax.broadcasted_iota(jnp.int32, (CELLS, 128), 1) // HEAD_DIM) % 2 == 0
    zero = jnp.zeros((CELLS, 128), BF16)
    for duo in range(cells // 128):
        both = slice(duo * 128, (duo + 1) * 128)
        for g in range(HEADS // group):
            part = slice(g * 256, (g + 1) * 256)
            lanes = slice(g * group * CELLS, (g + 1) * group * CELLS)
            probs = []
            for w in (2 * duo, 2 * duo + 1):
                span = slice(w * CELLS, (w + 1) * CELLS)
                query = jnp.concatenate([q_ref[span, part]] * group, axis=0) * mask_ref[...]
                scores = lax.dot_general(
                    k_ref[span, part], query, (((1,), (1,)), ((), ())), preferred_element_type=F32
                )
                scores = scores * SCORE_SCALE + bias_ref[:, lanes]
                scores = jnp.exp2(scores - jnp.max(scores, axis=0, keepdims=True))
                weight = 1.0 / jnp.sum(scores, axis=0, keepdims=True)
                probs.append((scores * weight).astype(BF16))
            for quad in range(group // 4):
                outs = []
                for pair in (2 * quad, 2 * quad + 1):
                    c = slice(pair * 128, (pair + 1) * 128)
                    right = jnp.concatenate(
                        [
                            jnp.concatenate([probs[0][:, c], zero], axis=1),
                            jnp.concatenate([zero, probs[1][:, c]], axis=1),
                        ],
                        axis=0,
                    )
                    first = g * 256 + pair * 64
                    outs.append(
                        jnp.dot(
                            vt_ref[first : first + 64, both], right, preferred_element_type=F32
                        )
                    )
                first = g * 256 + quad * 128
                for k in range(2):
                    turned = jnp.concatenate([o[:, k * 128 : (k + 1) * 128] for o in outs], axis=0)
                    turned = turned.T
                    picked = jnp.where(even, turned[:CELLS], turned[CELLS:])
                    row = (2 * duo + k) * CELLS
                    o_ref[row : row + CELLS, first : first + 128] = picked.astype(BF16)
    return stream + jnp.dot(o_ref[...], out_weight_ref[...], preferred_element_type=F32)


def block_kernel(
    act_ref, x_ref, part_ref, up_ref, proj_ref, gain_ref, in_ref, out_weight_ref, bias_ref,
    out_ref, gate_ref, *scratch,
):
    cols, rows, expanded = act_ref.shape
    channels = x_ref.shape[2]

    @pl.when(pl.program_id(0) == 0)
    def _():
        squeezed = jnp.broadcast_to(part_ref[...], (8, part_ref.shape[1]))
        squeezed = squeezed * jax.nn.sigmoid(squeezed)
        gate = jnp.dot(
            squeezed,
            up_ref[...].astype(F32),
            precision=lax.Precision.HIGHEST,
            preferred_element_type=F32,
        )
        gate_ref[...] = jax.nn.sigmoid(gate) * ROOT_HALF
        prepare(in_ref, scratch[0], scratch[1])

    gated = act_ref[...].reshape(cols * rows, expanded).astype(F32) * gate_ref[0:1]
    first = jnp.dot(gated.astype(BF16), proj_ref[...], preferred_element_type=F32)
    first = first.reshape(cols, rows, channels) + x_ref[...].astype(F32)
    first = first.astype(BF16).astype(F32)
    windows = rows // WIN
    stream = jnp.concatenate(
        [first[:, a * WIN : (a + 1) * WIN].reshape(CELLS, channels) for a in range(windows)],
        axis=0,
    )
    second = attend(
        stream, gain_ref, in_ref, out_weight_ref, bias_ref, scratch
    ).reshape(windows, cols, WIN, channels)
    second = jnp.concatenate([second[a] for a in range(windows)], axis=1)
    out_ref[...] = second.reshape(out_ref.shape).astype(BF16)


def grid_kernel(
    s_ref, perm_ref, back_ref, gain_ref, in_ref, out_weight_ref, bias_ref, out_ref, *scratch,
):
    @pl.when(pl.program_id(0) == 0)
    def _():
        prepare(in_ref, scratch[0], scratch[1])

    cells = perm_ref.shape[0]
    channels = s_ref.shape[-1]
    incoming = s_ref[...].reshape(cells, channels)
    stream = jnp.dot(perm_ref[...], incoming, preferred_element_type=F32)
    result = attend(
        stream, gain_ref, in_ref, out_weight_ref, bias_ref, scratch
    ).astype(BF16)
    result = jnp.dot(back_ref[...], result, preferred_element_type=F32)
    out_ref[...] = result.astype(BF16).reshape(out_ref.shape)


def whole(shape):
    return pl.BlockSpec(shape, lambda *_: (0,) * len(shape), pipeline_mode=pl.Buffered(1))


def attention_scratch(cells, channels):
    return [
        pltpu.VMEM((channels, channels), BF16),
        pltpu.VMEM((256 // HEAD_DIM * CELLS, 256), BF16),
        pltpu.VMEM((cells, channels), BF16),
        pltpu.VMEM((cells, channels), BF16),
        pltpu.VMEM((channels, cells), BF16),
        pltpu.VMEM((cells, channels), BF16),
    ]


def block_stage(start, count, active, field, part, up, proj, params):
    cols, rows, channels = field.shape
    expanded = active.shape[2]
    cells = WIN * rows
    return pl.pallas_call(
        block_kernel,
        name="block_stage",
        grid=(count,),
        in_specs=[
            pl.BlockSpec((WIN, rows, expanded), lambda b: (b + start, 0, 0)),
            pl.BlockSpec((WIN, rows, channels), lambda b: (b + start, 0, 0)),
        ]
        + [whole(p.shape) for p in (part, up, proj, *params)],
        out_specs=pl.BlockSpec((WIN, 1, rows, channels), lambda b: (0, b, 0, 0)),
        out_shape=jax.ShapeDtypeStruct((WIN, count, rows, channels), BF16),
        scratch_shapes=[pltpu.VMEM((8, expanded), F32)] + attention_scratch(cells, channels),
        cost_estimate=pl.CostEstimate(
            flops=2 * count * cells * channels * (expanded + 4 * channels) * 4,
            bytes_accessed=8_000_000,
            transcendentals=0,
        ),
        compiler_params=pltpu.CompilerParams(vmem_limit_bytes=VMEM_BYTES),
    )(active, field, part, up, proj, *params)


def grid_stage(received, perm, back, params):
    _, count, rows, channels = received.shape
    cells = WIN * rows
    spec = pl.BlockSpec((WIN, 1, rows, channels), lambda b: (0, b, 0, 0))
    return pl.pallas_call(
        grid_kernel,
        name="grid_stage",
        grid=(count,),
        in_specs=[spec] + [whole(p.shape) for p in (perm, back, *params)],
        out_specs=spec,
        out_shape=jax.ShapeDtypeStruct(received.shape, BF16),
        scratch_shapes=attention_scratch(cells, channels),
        cost_estimate=pl.CostEstimate(
            flops=2 * count * cells * channels * 4 * channels * 4,
            bytes_accessed=6_000_000,
            transcendentals=0,
        ),
        compiler_params=pltpu.CompilerParams(vmem_limit_bytes=VMEM_BYTES),
    )(received, perm, back, *params)


def turned_bias(pos_table):
    position = jnp.arange(CELLS)
    row = position % WIN
    col = position // WIN
    index = (row[None, :] - row[:, None] + 7) * 15 + (col[None, :] - col[:, None] + 7)
    one_hot = (index[:, :, None] == jnp.arange(225)[None, None, :]).astype(F32)
    bias = jnp.einsum("jir,rh->jhi", one_hot, pos_table * LOG2E, precision=lax.Precision.HIGHEST)
    return bias.reshape(CELLS, HEADS * CELLS)


def attention_params(gain, in_weight, out_weight, pos_table):
    return gain.reshape(1, -1), in_weight, out_weight, turned_bias(pos_table)


def grid_order(rows):
    per = rows // WIN
    source = np.zeros(WIN * rows, np.int64)
    for a in range(per):
        for j in range(WIN):
            for i in range(WIN):
                source[(a * WIN + j) * WIN + i] = j * rows + i * per + a
    one_hot = source[:, None] == np.arange(WIN * rows)[None, :]
    return jnp.asarray(one_hot, BF16), jnp.asarray(one_hot.T, BF16)


def per_device(
    input_field,
    expand_weight,
    expand_bias,
    depth_weight,
    depth_bias,
    squeeze_down,
    squeeze_up,
    project_weight,
    block_gain,
    block_in_weight,
    block_out_weight,
    block_table,
    grid_gain,
    grid_in_weight,
    grid_out_weight,
    grid_table,
):
    rows, cols, channels = input_field.shape
    count = lax.axis_size("lon")
    per = count // WIN
    groups = [[j * per + r for j in range(WIN)] for r in range(per)]
    field = jnp.swapaxes(input_field, 0, 1)
    before = lax.ppermute(field[-1:], "lon", [(i, (i + 1) % count) for i in range(count)])
    after = lax.ppermute(field[:1], "lon", [((i + 1) % count, i) for i in range(count)])
    rimmed = jnp.concatenate([before, field, after], axis=0)
    active, part = mbconv(
        rimmed, expand_weight, expand_bias, depth_weight, depth_bias, squeeze_down
    )
    parts = lax.all_to_all(
        jnp.broadcast_to(part[None, :1], (count, 1, part.shape[1])), "lon", 0, 0, tiled=True
    )
    part = jnp.sum(parts, axis=0) * (ROOT_HALF / (rows * cols * count))
    perm, back = grid_order(rows)
    block_params = attention_params(block_gain, block_in_weight, block_out_weight, block_table)
    grid_params = attention_params(grid_gain, grid_in_weight, grid_out_weight, grid_table)
    exchange = functools.partial(
        lax.all_to_all,
        axis_name="lon",
        split_axis=0,
        concat_axis=0,
        axis_index_groups=groups,
        tiled=True,
    )
    results = []
    start = 0
    total = cols // WIN
    for size in CHUNKS if sum(CHUNKS) == total else (total,):
        sent = block_stage(
            start, size, active, field, part, squeeze_up, project_weight, block_params
        )
        start += size
        result = grid_stage(exchange(sent), perm, back, grid_params)
        results.append(exchange(result))
    merged = jnp.concatenate(results, axis=1)
    return merged.transpose(2, 1, 0, 3).reshape(rows, cols, channels)


def solution(mesh):
    return jax.shard_map(
        per_device,
        mesh=mesh,
        in_specs=(P("groups", "lon", None),) + (P(),) * 15,
        out_specs=P("groups", "lon", None),
        check_vma=False,
    )
```

```python
import functools

import jax
import jax.numpy as jnp
import numpy as np
from jax import lax
from jax.experimental import pallas as pl
from jax.experimental.pallas import tpu as pltpu
from jax.sharding import PartitionSpec as P

HEADS = 16
HEAD_DIM = 32
WIN = 8
CELLS = WIN * WIN
CHUNKS = ((2, True), (2, True))
LANES = 512
SUB = 256
VMEM_BYTES = 60 << 20
ROOT_HALF = 0.7071067811865476
LOG2E = 1.4426950408889634
SCORE_SCALE = HEAD_DIM ** (-0.5) * LOG2E
BF16 = jnp.bfloat16
F32 = jnp.float32


def whole(shape):
    return pl.BlockSpec(shape, lambda *_: (0,) * len(shape), pipeline_mode=pl.Buffered(1))


def double_gelu(half):
    return half + half * lax.erf(half)


def mbconv_kernel(
    x_ref, before_ref, after_ref, w_ref, b_ref, dw_ref, db_ref, down_ref, shift_ref,
    act_ref, part_ref, total_ref, tap_ref, *hidden_refs,
):
    out_cols, rows, channels = x_ref.shape
    lanes = w_ref.shape[1]
    sub = hidden_refs[0].shape[2]
    half = out_cols // 2
    pieces = 2
    piece = half + 1
    shift = shift_ref[...]
    for k in range(9):
        tap_ref[k] = jnp.broadcast_to(dw_ref[k : k + 1] * 0.5, (16, lanes)).astype(BF16)

    def expand(s, i):
        span = slice(s * sub, (s + 1) * sub)
        if i == 0:
            cells = jnp.concatenate([before_ref[...], x_ref[:half]], axis=0)
        else:
            cells = jnp.concatenate([x_ref[half:], after_ref[...]], axis=0)
        cells = cells.reshape(piece * rows, channels)
        hidden = jnp.dot(cells, w_ref[:, span], preferred_element_type=F32)
        hidden = double_gelu(hidden * ROOT_HALF + b_ref[:, span] * ROOT_HALF)
        hidden_refs[s][i * piece : (i + 1) * piece] = hidden.astype(BF16).reshape(piece, rows, sub)

    def depth(s, c, total):
        span = slice(s * sub, (s + 1) * sub)
        near = [hidden_refs[s][c + k].reshape(rows // 16, 16, sub) for k in range(3)]
        sums = []
        for r in range(3):
            terms = [near[k] * tap_ref[3 * r + k, :, span][None] for k in range(3)]
            sums.append((terms[0] + terms[1] + terms[2]).reshape(rows, sub))
        summed = jnp.dot(shift, jnp.concatenate(sums, axis=0), preferred_element_type=F32)
        active = double_gelu(summed + db_ref[:, span] * ROOT_HALF)
        act_ref[c, :, span] = active.astype(BF16)
        return total + active.reshape(rows // 8, 8, sub).sum(0)

    for i in range(pieces):
        expand(0, i)
    for s in range(len(hidden_refs)):
        total = jnp.zeros((8, sub), F32)
        for i in range(pieces):
            if s + 1 < len(hidden_refs):
                expand(s + 1, i)
            for c in range(i * out_cols // pieces, (i + 1) * out_cols // pieces):
                total = depth(s, c, total)
        total_ref[:, s * sub : (s + 1) * sub] = total
    pooled = jnp.sum(total_ref[...], axis=0, keepdims=True)
    part = jnp.dot(
        jnp.broadcast_to(pooled, (8, lanes)),
        down_ref[...].astype(F32),
        precision=lax.Precision.HIGHEST,
        preferred_element_type=F32,
    )[None]

    @pl.when(pl.program_id(0) == 0)
    def _():
        part_ref[...] = jnp.broadcast_to(part, part_ref.shape)

    @pl.when(pl.program_id(0) > 0)
    def _():
        part_ref[...] += part


def row_shifts(rows):
    shift = np.zeros((rows, 3 * rows), np.float32)
    for offset in range(3):
        for row in range(rows):
            if 0 <= row + offset - 1 < rows:
                shift[row, offset * rows + row + offset - 1] = 1.0
    return jnp.asarray(shift, BF16)


def mbconv(
    count, field, before, after, expand_weight, expand_bias, depth_weight, depth_bias, squeeze_down
):
    cols, rows, channels = field.shape
    expanded = expand_weight.shape[1]
    squeeze = squeeze_down.shape[1]
    return pl.pallas_call(
        mbconv_kernel,
        name="mbconv",
        grid=(expanded // LANES,),
        in_specs=[
            whole(field.shape),
            whole(before.shape),
            whole(after.shape),
            pl.BlockSpec((channels, LANES), lambda i: (0, i)),
            pl.BlockSpec((1, LANES), lambda i: (0, i)),
            pl.BlockSpec((9, LANES), lambda i: (0, i)),
            pl.BlockSpec((1, LANES), lambda i: (0, i)),
            pl.BlockSpec((LANES, squeeze), lambda i: (i, 0)),
            pl.BlockSpec((rows, 3 * rows), lambda i: (0, 0)),
        ],
        out_specs=[
            pl.BlockSpec((cols, rows, LANES), lambda i: (0, 0, i)),
            pl.BlockSpec((count, 8, squeeze), lambda i: (0, 0, 0)),
        ],
        out_shape=[
            jax.ShapeDtypeStruct((cols, rows, expanded), BF16),
            jax.ShapeDtypeStruct((count, 8, squeeze), F32),
        ],
        scratch_shapes=[pltpu.VMEM((8, LANES), F32), pltpu.VMEM((9, 16, LANES), BF16)]
        + [pltpu.VMEM((cols + 2, rows, SUB), BF16)] * (LANES // SUB),
        cost_estimate=pl.CostEstimate(
            flops=2 * cols * rows * channels * expanded * 4,
            bytes_accessed=20_000_000,
            transcendentals=0,
        ),
        compiler_params=pltpu.CompilerParams(vmem_limit_bytes=VMEM_BYTES),
    )(
        field,
        before,
        after,
        expand_weight,
        expand_bias.reshape(1, -1),
        depth_weight,
        depth_bias.reshape(1, -1),
        squeeze_down,
        row_shifts(rows),
    )


def prepare(in_ref, wv_ref, mask_ref):
    channels = in_ref.shape[0]
    wv_ref[...] = in_ref[:, 2 * channels :].T
    head = lax.broadcasted_iota(jnp.int32, mask_ref.shape, 0) // CELLS
    lane = lax.broadcasted_iota(jnp.int32, mask_ref.shape, 1) // HEAD_DIM
    mask_ref[...] = (head == lane).astype(F32).astype(BF16)


def attend(stream, gain_ref, in_ref, out_weight_ref, bias_ref, scratch):
    wv_ref, mask_ref, q_ref, k_ref, vt_ref, o_ref = scratch
    cells, channels = stream.shape
    average = jnp.mean(stream, axis=-1, keepdims=True)
    centred = stream - average
    variance = jnp.mean(centred * centred, axis=-1, keepdims=True)
    normed = (centred * lax.rsqrt(variance + 1e-05) * gain_ref[...]).astype(BF16)
    q_ref[...] = jnp.dot(normed, in_ref[:, :channels], preferred_element_type=F32).astype(BF16)
    k_ref[...] = jnp.dot(
        normed, in_ref[:, channels : 2 * channels], preferred_element_type=F32
    ).astype(BF16)
    vt_ref[...] = lax.dot_general(
        wv_ref[...], normed, (((1,), (1,)), ((), ())), preferred_element_type=F32
    ).astype(BF16)
    group = 256 // HEAD_DIM
    even = (lax.broadcasted_iota(jnp.int32, (CELLS, 128), 1) // HEAD_DIM) % 2 == 0
    zero = jnp.zeros((CELLS, 128), BF16)
    for duo in range(cells // 128):
        both = slice(duo * 128, (duo + 1) * 128)
        for g in range(HEADS // group):
            part = slice(g * 256, (g + 1) * 256)
            lanes = slice(g * group * CELLS, (g + 1) * group * CELLS)
            probs = []
            for w in (2 * duo, 2 * duo + 1):
                span = slice(w * CELLS, (w + 1) * CELLS)
                query = jnp.concatenate([q_ref[span, part]] * group, axis=0) * mask_ref[...]
                scores = lax.dot_general(
                    k_ref[span, part], query, (((1,), (1,)), ((), ())), preferred_element_type=F32
                )
                scores = scores * SCORE_SCALE + bias_ref[:, lanes]
                scores = jnp.exp2(scores - jnp.max(scores, axis=0, keepdims=True))
                weight = 1.0 / jnp.sum(scores, axis=0, keepdims=True)
                probs.append((scores * weight).astype(BF16))
            for quad in range(group // 4):
                outs = []
                for pair in (2 * quad, 2 * quad + 1):
                    c = slice(pair * 128, (pair + 1) * 128)
                    right = jnp.concatenate(
                        [
                            jnp.concatenate([probs[0][:, c], zero], axis=1),
                            jnp.concatenate([zero, probs[1][:, c]], axis=1),
                        ],
                        axis=0,
                    )
                    first = g * 256 + pair * 64
                    outs.append(
                        jnp.dot(
                            vt_ref[first : first + 64, both], right, preferred_element_type=F32
                        )
                    )
                first = g * 256 + quad * 128
                for k in range(2):
                    turned = jnp.concatenate([o[:, k * 128 : (k + 1) * 128] for o in outs], axis=0)
                    turned = turned.T
                    picked = jnp.where(even, turned[:CELLS], turned[CELLS:])
                    row = (2 * duo + k) * CELLS
                    o_ref[row : row + CELLS, first : first + 128] = picked.astype(BF16)
    return stream + jnp.dot(o_ref[...], out_weight_ref[...], preferred_element_type=F32)


def block_kernel(
    scale, split, me_ref, act_ref, x_ref, part_ref, up_ref, proj_ref, gain_ref, in_ref,
    out_weight_ref, bias_ref, *refs,
):
    outs, (gate_ref, sent_ref, *scratch) = (refs[:WIN], refs[WIN:]) if split else (refs[:1], refs[1:])
    cols, rows, expanded = act_ref.shape
    channels = x_ref.shape[2]

    @pl.when(pl.program_id(0) == 0)
    def _():
        squeezed = jnp.sum(part_ref[...], axis=0) * scale
        squeezed = squeezed * jax.nn.sigmoid(squeezed)
        gate = jnp.dot(
            squeezed,
            up_ref[...].astype(F32),
            precision=lax.Precision.HIGHEST,
            preferred_element_type=F32,
        )
        gate_ref[...] = jax.nn.sigmoid(gate) * ROOT_HALF
        prepare(in_ref, scratch[0], scratch[1])

    gated = act_ref[...].reshape(cols * rows, expanded).astype(F32) * gate_ref[0:1]
    first = jnp.dot(gated.astype(BF16), proj_ref[...], preferred_element_type=F32)
    first = first.reshape(cols, rows, channels) + x_ref[...].astype(F32)
    first = first.astype(BF16).astype(F32)
    windows = rows // WIN
    stream = jnp.concatenate(
        [first[:, a * WIN : (a + 1) * WIN].reshape(CELLS, channels) for a in range(windows)],
        axis=0,
    )
    second = attend(stream, gain_ref, in_ref, out_weight_ref, bias_ref, scratch)
    second = second.reshape(windows, cols, WIN, channels)
    second = jnp.concatenate([second[a] for a in range(windows)], axis=1).astype(BF16)
    deliver(second, me_ref, outs, sent_ref)


def deliver(pieces, me_ref, outs, sent_ref):
    if len(outs) == 1:
        outs[0][:, 0] = pieces
        return
    sent_ref[...] = pieces
    for s in range(WIN):
        outs[s][0] = sent_ref[me_ref[0] ^ s]


def gathered(ins):
    if len(ins) == 1:
        return ins[0][...].reshape(-1, ins[0].shape[-1])
    return jnp.concatenate([ref[0] for ref in ins], axis=0)


def grid_kernel(split, me_ref, *refs):
    n = WIN if split else 1
    ins, refs = refs[:n], refs[n:]
    perm_ref, gain_ref, in_ref, out_weight_ref, bias_ref = refs[:5]
    outs, (sent_ref, *scratch) = refs[5 : 5 + n], refs[5 + n :]

    @pl.when(pl.program_id(0) == 0)
    def _():
        prepare(in_ref, scratch[0], scratch[1])

    stream = jnp.dot(perm_ref[0], gathered(ins), preferred_element_type=F32)
    result = attend(stream, gain_ref, in_ref, out_weight_ref, bias_ref, scratch)
    channels = result.shape[1]
    result = result.reshape(-1, WIN, WIN, channels)
    result = jnp.concatenate([result[a] for a in range(result.shape[0])], axis=1).astype(BF16)
    deliver(result, me_ref, outs, sent_ref)


def merge_kernel(split, me_ref, *refs):
    n = WIN if split else 1
    ins, perm_ref, out_ref = refs[:n], refs[n], refs[-1]
    cells = jnp.dot(perm_ref[0], gathered(ins), preferred_element_type=F32)
    out_ref[...] = cells.reshape(out_ref.shape).astype(BF16)


def attention_scratch(cells, channels):
    return [
        pltpu.VMEM((channels, channels), BF16),
        pltpu.VMEM((256 // HEAD_DIM * CELLS, 256), BF16),
        pltpu.VMEM((cells, channels), BF16),
        pltpu.VMEM((cells, channels), BF16),
        pltpu.VMEM((channels, cells), BF16),
        pltpu.VMEM((cells, channels), BF16),
    ]


def partner_specs(split, rows, channels):
    if split:
        return [pl.BlockSpec((1, rows, channels), lambda b, me: (b, 0, 0))] * WIN
    return [pl.BlockSpec((WIN, 1, rows, channels), lambda b, me: (0, b, 0, 0))]


def partner_shapes(split, count, rows, channels):
    if split:
        return [jax.ShapeDtypeStruct((count, rows, channels), BF16)] * WIN
    return [jax.ShapeDtypeStruct((WIN, count, rows, channels), BF16)]


def block_stage(split, start, count, scale, me, active, field, parts, up, proj, params):
    cols, rows, channels = field.shape
    expanded = active.shape[2]
    cells = WIN * rows
    return pl.pallas_call(
        functools.partial(block_kernel, scale, split),
        name="block_stage",
        grid_spec=pltpu.PrefetchScalarGridSpec(
            num_scalar_prefetch=1,
            grid=(count,),
            in_specs=[
                pl.BlockSpec((WIN, rows, expanded), lambda b, me: (b + start, 0, 0)),
                pl.BlockSpec((WIN, rows, channels), lambda b, me: (b + start, 0, 0)),
            ]
            + [whole(p.shape) for p in (parts, up, proj, *params)],
            out_specs=partner_specs(split, rows, channels),
            scratch_shapes=[
                pltpu.VMEM((8, expanded), F32),
                pltpu.VMEM((WIN, rows, channels), BF16),
            ]
            + attention_scratch(cells, channels),
        ),
        out_shape=partner_shapes(split, count, rows, channels),
        cost_estimate=pl.CostEstimate(
            flops=2 * count * cells * channels * (expanded + 4 * channels) * 4,
            bytes_accessed=8_000_000,
            transcendentals=0,
        ),
        compiler_params=pltpu.CompilerParams(vmem_limit_bytes=VMEM_BYTES),
    )(me, active, field, parts, up, proj, *params)


def grid_stage(split, me, received, perm, params):
    count, rows, channels = received[0].shape[-3:]
    cells = WIN * rows
    return pl.pallas_call(
        functools.partial(grid_kernel, split),
        name="grid_stage",
        grid_spec=pltpu.PrefetchScalarGridSpec(
            num_scalar_prefetch=1,
            grid=(count,),
            in_specs=partner_specs(split, rows, channels)
            + [pl.BlockSpec((1, cells, cells), lambda b, me: (me[0], 0, 0))]
            + [whole(p.shape) for p in params],
            out_specs=partner_specs(split, rows, channels),
            scratch_shapes=[pltpu.VMEM((WIN, rows, channels), BF16)]
            + attention_scratch(cells, channels),
        ),
        out_shape=partner_shapes(split, count, rows, channels),
        cost_estimate=pl.CostEstimate(
            flops=2 * count * cells * channels * 4 * channels * 4,
            bytes_accessed=6_000_000,
            transcendentals=0,
        ),
        compiler_params=pltpu.CompilerParams(vmem_limit_bytes=VMEM_BYTES),
    )(me, *received, perm, *params)


def merge_stage(split, start, total, me, received, perm, merged):
    count, rows, channels = received[0].shape[-3:]
    cells = WIN * rows
    n = len(received)
    return pl.pallas_call(
        functools.partial(merge_kernel, split),
        name="merge_stage",
        grid_spec=pltpu.PrefetchScalarGridSpec(
            num_scalar_prefetch=1,
            grid=(count,),
            in_specs=partner_specs(split, rows, channels)
            + [pl.BlockSpec((1, cells, cells), lambda b, me: (me[0], 0, 0))]
            + [pl.BlockSpec(memory_space=pl.ANY)] * (merged is not None),
            out_specs=pl.BlockSpec((rows, WIN, channels), lambda b, me: (0, b + start, 0)),
        ),
        out_shape=jax.ShapeDtypeStruct((rows, total * WIN, channels), BF16),
        input_output_aliases={} if merged is None else {n + 2: 0},
        cost_estimate=pl.CostEstimate(
            flops=2 * count * cells * cells * channels,
            bytes_accessed=2_000_000,
            transcendentals=0,
        ),
        compiler_params=pltpu.CompilerParams(vmem_limit_bytes=VMEM_BYTES),
    )(me, *received, perm, *([] if merged is None else [merged]))


def turned_bias(pos_table):
    position = jnp.arange(CELLS)
    row = position % WIN
    col = position // WIN
    index = (row[None, :] - row[:, None] + 7) * 15 + (col[None, :] - col[:, None] + 7)
    one_hot = (index[:, :, None] == jnp.arange(225)[None, None, :]).astype(F32)
    bias = jnp.einsum("jir,rh->jhi", one_hot, pos_table * LOG2E, precision=lax.Precision.HIGHEST)
    return bias.reshape(CELLS, HEADS * CELLS)


def attention_params(gain, in_weight, out_weight, pos_table):
    return gain.reshape(1, -1), in_weight, out_weight, turned_bias(pos_table)


def cell_orders(rows):
    per = rows // WIN
    cells = WIN * rows
    into = np.zeros((WIN, cells, cells), np.float32)
    back = np.zeros((WIN, cells, cells), np.float32)
    a, j, i = np.meshgrid(np.arange(per), np.arange(WIN), np.arange(WIN), indexing="ij")
    for m in range(WIN):
        into[m, (a * WIN + j) * WIN + i, (m ^ j) * rows + i * per + a] = 1.0
        back[m, (i * per + a) * WIN + j, (m ^ j) * rows + a * WIN + i] = 1.0
    return jnp.asarray(into, BF16), jnp.asarray(back, BF16)


def per_device(
    input_field,
    expand_weight,
    expand_bias,
    depth_weight,
    depth_bias,
    squeeze_down,
    squeeze_up,
    project_weight,
    block_gain,
    block_in_weight,
    block_out_weight,
    block_table,
    grid_gain,
    grid_in_weight,
    grid_out_weight,
    grid_table,
):
    rows, cols, channels = input_field.shape
    count = lax.axis_size("lon")
    per = count // WIN
    groups = [[j * per + r for j in range(WIN)] for r in range(per)]
    place = lax.axis_index("lon") // per
    places = {True: place.reshape(1).astype(jnp.int32), False: jnp.zeros((1,), jnp.int32)}
    before = lax.ppermute(
        jnp.swapaxes(input_field[:, -1:], 0, 1),
        "lon",
        [(i, (i + 1) % count) for i in range(count)],
    )
    after = lax.ppermute(
        jnp.swapaxes(input_field[:, :1], 0, 1),
        "lon",
        [((i + 1) % count, i) for i in range(count)],
    )
    field = jnp.swapaxes(input_field, 0, 1)
    active, part = mbconv(
        count, field, before, after, expand_weight, expand_bias, depth_weight, depth_bias,
        squeeze_down,
    )
    parts = lax.all_to_all(part, "lon", 0, 0, tiled=True)
    scale = ROOT_HALF / (rows * cols * count)
    into, back = cell_orders(rows)
    block_params = attention_params(block_gain, block_in_weight, block_out_weight, block_table)
    grid_params = attention_params(grid_gain, grid_in_weight, grid_out_weight, grid_table)

    def exchange(split, pieces):
        if not split:
            return [
                lax.all_to_all(
                    pieces[0], "lon", 0, 0, axis_index_groups=groups, tiled=True
                )
            ]
        return [pieces[0]] + [
            lax.ppermute(
                pieces[s],
                "lon",
                [(j * per + r, (j ^ s) * per + r) for j in range(WIN) for r in range(per)],
            )
            for s in range(1, WIN)
        ]

    total = cols // WIN
    chunks = CHUNKS if sum(c[0] for c in CHUNKS) == total else ((total, False),)
    starts = [sum(c[0] for c in chunks[:k]) for k in range(len(chunks))]
    sent = [
        block_stage(
            split, start, size, scale, places[split], active, field, parts, squeeze_up,
            project_weight, block_params,
        )
        for start, (size, split) in zip(starts, chunks)
    ]
    received = [exchange(split, pieces) for pieces, (_, split) in zip(sent, chunks)]
    results = []
    for k, (_, split) in enumerate(chunks):
        pieces = received[k]
        if k + 1 < len(chunks):
            pieces, _ = lax.optimization_barrier((pieces, sent[k + 1][0]))
        results.append(grid_stage(split, places[split], pieces, into, grid_params))
    merged = None
    for start, result, (_, split) in zip(starts, results, chunks):
        merged = merge_stage(
            split, start, total, places[split], exchange(split, result), back, merged
        )
    return merged


def solution(mesh):
    return jax.shard_map(
        per_device,
        mesh=mesh,
        in_specs=(P("groups", "lon", None),) + (P(),) * 15,
        out_specs=P("groups", "lon", None),
        check_vma=False,
    )
```

```python
import functools

import jax
import jax.numpy as jnp
import numpy as np
from jax import lax
from jax.experimental import pallas as pl
from jax.experimental.pallas import tpu as pltpu
from jax.sharding import PartitionSpec as P

HEADS = 16
HEAD_DIM = 32
WIN = 8
CELLS = WIN * WIN
CHUNKS = ((2, False, True), (2, False, True))
LANES = 512
SUB = 256
VMEM_BYTES = 60 << 20
ROOT_HALF = 0.7071067811865476
LOG2E = 1.4426950408889634
SCORE_SCALE = HEAD_DIM ** (-0.5) * LOG2E
BF16 = jnp.bfloat16
F32 = jnp.float32


def whole(shape):
    return pl.BlockSpec(shape, lambda *_: (0,) * len(shape), pipeline_mode=pl.Buffered(1))


def double_gelu(half):
    return half + half * lax.erf(half)


def mbconv_kernel(
    x_ref, before_ref, after_ref, w_ref, b_ref, dw_ref, db_ref, down_ref, shift_ref,
    act_ref, part_ref, total_ref, tap_ref, *hidden_refs,
):
    out_cols, rows, channels = x_ref.shape
    lanes = w_ref.shape[1]
    sub = hidden_refs[0].shape[2]
    half = out_cols // 2
    pieces = 2
    piece = half + 1
    shift = shift_ref[...]
    for k in range(9):
        tap_ref[k] = jnp.broadcast_to(dw_ref[k : k + 1] * 0.5, (16, lanes)).astype(BF16)

    def expand(s, i):
        span = slice(s * sub, (s + 1) * sub)
        if i == 0:
            cells = jnp.concatenate([before_ref[...], x_ref[:half]], axis=0)
        else:
            cells = jnp.concatenate([x_ref[half:], after_ref[...]], axis=0)
        cells = cells.reshape(piece * rows, channels)
        hidden = jnp.dot(cells, w_ref[:, span], preferred_element_type=F32)
        hidden = double_gelu(hidden * ROOT_HALF + b_ref[:, span] * ROOT_HALF)
        hidden_refs[s][i * piece : (i + 1) * piece] = hidden.astype(BF16).reshape(piece, rows, sub)

    def depth(s, c, total):
        span = slice(s * sub, (s + 1) * sub)
        near = [hidden_refs[s][c + k].reshape(rows // 16, 16, sub) for k in range(3)]
        sums = []
        for r in range(3):
            terms = [near[k] * tap_ref[3 * r + k, :, span][None] for k in range(3)]
            sums.append((terms[0] + terms[1] + terms[2]).reshape(rows, sub))
        summed = jnp.dot(shift, jnp.concatenate(sums, axis=0), preferred_element_type=F32)
        active = double_gelu(summed + db_ref[:, span] * ROOT_HALF)
        act_ref[c, :, span] = active.astype(BF16)
        return total + active.reshape(rows // 8, 8, sub).sum(0)

    for i in range(pieces):
        expand(0, i)
    for s in range(len(hidden_refs)):
        total = jnp.zeros((8, sub), F32)
        for i in range(pieces):
            if s + 1 < len(hidden_refs):
                expand(s + 1, i)
            for c in range(i * out_cols // pieces, (i + 1) * out_cols // pieces):
                total = depth(s, c, total)
        total_ref[:, s * sub : (s + 1) * sub] = total
    pooled = jnp.sum(total_ref[...], axis=0, keepdims=True)
    part = jnp.dot(
        jnp.broadcast_to(pooled, (8, lanes)),
        down_ref[...].astype(F32),
        precision=lax.Precision.HIGHEST,
        preferred_element_type=F32,
    )[None]

    @pl.when(pl.program_id(0) == 0)
    def _():
        part_ref[...] = jnp.broadcast_to(part, part_ref.shape)

    @pl.when(pl.program_id(0) > 0)
    def _():
        part_ref[...] += part


def row_shifts(rows):
    shift = np.zeros((rows, 3 * rows), np.float32)
    for offset in range(3):
        for row in range(rows):
            if 0 <= row + offset - 1 < rows:
                shift[row, offset * rows + row + offset - 1] = 1.0
    return jnp.asarray(shift, BF16)


def mbconv(
    count, field, before, after, expand_weight, expand_bias, depth_weight, depth_bias, squeeze_down
):
    cols, rows, channels = field.shape
    expanded = expand_weight.shape[1]
    squeeze = squeeze_down.shape[1]
    return pl.pallas_call(
        mbconv_kernel,
        name="mbconv",
        grid=(expanded // LANES,),
        in_specs=[
            whole(field.shape),
            whole(before.shape),
            whole(after.shape),
            pl.BlockSpec((channels, LANES), lambda i: (0, i)),
            pl.BlockSpec((1, LANES), lambda i: (0, i)),
            pl.BlockSpec((9, LANES), lambda i: (0, i)),
            pl.BlockSpec((1, LANES), lambda i: (0, i)),
            pl.BlockSpec((LANES, squeeze), lambda i: (i, 0)),
            pl.BlockSpec((rows, 3 * rows), lambda i: (0, 0)),
        ],
        out_specs=[
            pl.BlockSpec((cols, rows, LANES), lambda i: (0, 0, i)),
            pl.BlockSpec((count, 8, squeeze), lambda i: (0, 0, 0)),
        ],
        out_shape=[
            jax.ShapeDtypeStruct((cols, rows, expanded), BF16),
            jax.ShapeDtypeStruct((count, 8, squeeze), F32),
        ],
        scratch_shapes=[pltpu.VMEM((8, LANES), F32), pltpu.VMEM((9, 16, LANES), BF16)]
        + [pltpu.VMEM((cols + 2, rows, SUB), BF16)] * (LANES // SUB),
        cost_estimate=pl.CostEstimate(
            flops=2 * cols * rows * channels * expanded * 4,
            bytes_accessed=20_000_000,
            transcendentals=0,
        ),
        compiler_params=pltpu.CompilerParams(vmem_limit_bytes=VMEM_BYTES),
    )(
        field,
        before,
        after,
        expand_weight,
        expand_bias.reshape(1, -1),
        depth_weight,
        depth_bias.reshape(1, -1),
        squeeze_down,
        row_shifts(rows),
    )


def prepare(in_ref, wv_ref, mask_ref):
    channels = in_ref.shape[0]
    wv_ref[...] = in_ref[:, 2 * channels :].T
    head = lax.broadcasted_iota(jnp.int32, mask_ref.shape, 0) // CELLS
    lane = lax.broadcasted_iota(jnp.int32, mask_ref.shape, 1) // HEAD_DIM
    mask_ref[...] = (head == lane).astype(F32).astype(BF16)


def attend(stream, gain_ref, in_ref, out_weight_ref, bias_ref, scratch):
    wv_ref, mask_ref, q_ref, k_ref, vt_ref, o_ref = scratch
    cells, channels = stream.shape
    average = jnp.mean(stream, axis=-1, keepdims=True)
    centred = stream - average
    variance = jnp.mean(centred * centred, axis=-1, keepdims=True)
    normed = (centred * lax.rsqrt(variance + 1e-05) * gain_ref[...]).astype(BF16)
    q_ref[...] = jnp.dot(normed, in_ref[:, :channels], preferred_element_type=F32).astype(BF16)
    k_ref[...] = jnp.dot(
        normed, in_ref[:, channels : 2 * channels], preferred_element_type=F32
    ).astype(BF16)
    vt_ref[...] = lax.dot_general(
        wv_ref[...], normed, (((1,), (1,)), ((), ())), preferred_element_type=F32
    ).astype(BF16)
    group = 256 // HEAD_DIM
    even = (lax.broadcasted_iota(jnp.int32, (CELLS, 128), 1) // HEAD_DIM) % 2 == 0
    zero = jnp.zeros((CELLS, 128), BF16)
    for duo in range(cells // 128):
        both = slice(duo * 128, (duo + 1) * 128)
        for g in range(HEADS // group):
            part = slice(g * 256, (g + 1) * 256)
            lanes = slice(g * group * CELLS, (g + 1) * group * CELLS)
            probs = []
            for w in (2 * duo, 2 * duo + 1):
                span = slice(w * CELLS, (w + 1) * CELLS)
                query = jnp.concatenate([q_ref[span, part]] * group, axis=0) * mask_ref[...]
                scores = lax.dot_general(
                    k_ref[span, part], query, (((1,), (1,)), ((), ())), preferred_element_type=F32
                )
                scores = scores * SCORE_SCALE + bias_ref[:, lanes]
                scores = jnp.exp2(scores - jnp.max(scores, axis=0, keepdims=True))
                weight = 1.0 / jnp.sum(scores, axis=0, keepdims=True)
                probs.append((scores * weight).astype(BF16))
            for quad in range(group // 4):
                outs = []
                for pair in (2 * quad, 2 * quad + 1):
                    c = slice(pair * 128, (pair + 1) * 128)
                    right = jnp.concatenate(
                        [
                            jnp.concatenate([probs[0][:, c], zero], axis=1),
                            jnp.concatenate([zero, probs[1][:, c]], axis=1),
                        ],
                        axis=0,
                    )
                    first = g * 256 + pair * 64
                    outs.append(
                        jnp.dot(
                            vt_ref[first : first + 64, both], right, preferred_element_type=F32
                        )
                    )
                first = g * 256 + quad * 128
                for k in range(2):
                    turned = jnp.concatenate([o[:, k * 128 : (k + 1) * 128] for o in outs], axis=0)
                    turned = turned.T
                    picked = jnp.where(even, turned[:CELLS], turned[CELLS:])
                    row = (2 * duo + k) * CELLS
                    o_ref[row : row + CELLS, first : first + 128] = picked.astype(BF16)
    return stream + jnp.dot(o_ref[...], out_weight_ref[...], preferred_element_type=F32)


def block_kernel(
    scale, split, me_ref, act_ref, x_ref, part_ref, up_ref, proj_ref, gain_ref, in_ref,
    out_weight_ref, bias_ref, *refs,
):
    outs, (gate_ref, sent_ref, *scratch) = (refs[:WIN], refs[WIN:]) if split else (refs[:1], refs[1:])
    cols, rows, expanded = act_ref.shape
    channels = x_ref.shape[2]

    @pl.when(pl.program_id(0) == 0)
    def _():
        squeezed = jnp.sum(part_ref[...], axis=0) * scale
        squeezed = squeezed * jax.nn.sigmoid(squeezed)
        gate = jnp.dot(
            squeezed,
            up_ref[...].astype(F32),
            precision=lax.Precision.HIGHEST,
            preferred_element_type=F32,
        )
        gate_ref[...] = jax.nn.sigmoid(gate) * ROOT_HALF
        prepare(in_ref, scratch[0], scratch[1])

    gated = act_ref[...].reshape(cols * rows, expanded).astype(F32) * gate_ref[0:1]
    first = jnp.dot(gated.astype(BF16), proj_ref[...], preferred_element_type=F32)
    first = first.reshape(cols, rows, channels) + x_ref[...].astype(F32)
    first = first.astype(BF16).astype(F32)
    windows = rows // WIN
    stream = jnp.concatenate(
        [first[:, a * WIN : (a + 1) * WIN].reshape(CELLS, channels) for a in range(windows)],
        axis=0,
    )
    second = attend(stream, gain_ref, in_ref, out_weight_ref, bias_ref, scratch)
    second = second.reshape(windows, cols, WIN, channels)
    second = jnp.concatenate([second[a] for a in range(windows)], axis=1).astype(BF16)
    deliver(second, me_ref, outs, sent_ref)


def deliver(pieces, me_ref, outs, sent_ref):
    if len(outs) == 1:
        outs[0][:, 0] = pieces
        return
    sent_ref[...] = pieces
    for s in range(WIN):
        outs[s][0] = sent_ref[me_ref[0] ^ s]


def gathered(ins):
    if len(ins) == 1:
        return ins[0][...].reshape(-1, ins[0].shape[-1])
    return jnp.concatenate([ref[0] for ref in ins], axis=0)


def grid_kernel(split_in, split_out, me_ref, *refs):
    n = WIN if split_in else 1
    ins, refs = refs[:n], refs[n:]
    perm_ref, gain_ref, in_ref, out_weight_ref, bias_ref = refs[:5]
    n = WIN if split_out else 1
    outs, (sent_ref, *scratch) = refs[5 : 5 + n], refs[5 + n :]

    @pl.when(pl.program_id(0) == 0)
    def _():
        prepare(in_ref, scratch[0], scratch[1])

    stream = jnp.dot(perm_ref[...], gathered(ins), preferred_element_type=F32)
    result = attend(stream, gain_ref, in_ref, out_weight_ref, bias_ref, scratch)
    channels = result.shape[1]
    result = result.reshape(-1, WIN, WIN, channels)
    result = jnp.concatenate([result[a] for a in range(result.shape[0])], axis=1).astype(BF16)
    deliver(result, me_ref, outs, sent_ref)


def merge_kernel(split, me_ref, *refs):
    n = WIN if split else 1
    ins, perm_ref, out_ref = refs[:n], refs[n], refs[-1]
    cells = jnp.dot(perm_ref[...], gathered(ins), preferred_element_type=F32)
    out_ref[...] = cells.reshape(out_ref.shape).astype(BF16)


def attention_scratch(cells, channels):
    return [
        pltpu.VMEM((channels, channels), BF16),
        pltpu.VMEM((256 // HEAD_DIM * CELLS, 256), BF16),
        pltpu.VMEM((cells, channels), BF16),
        pltpu.VMEM((cells, channels), BF16),
        pltpu.VMEM((channels, cells), BF16),
        pltpu.VMEM((cells, channels), BF16),
    ]


def partner_specs(split, rows, channels):
    if split:
        return [pl.BlockSpec((1, rows, channels), lambda b, me: (b, 0, 0))] * WIN
    return [pl.BlockSpec((WIN, 1, rows, channels), lambda b, me: (0, b, 0, 0))]


def partner_shapes(split, count, rows, channels):
    if split:
        return [jax.ShapeDtypeStruct((count, rows, channels), BF16)] * WIN
    return [jax.ShapeDtypeStruct((WIN, count, rows, channels), BF16)]


def block_stage(split, start, count, scale, me, active, field, parts, up, proj, params):
    cols, rows, channels = field.shape
    expanded = active.shape[2]
    cells = WIN * rows
    return pl.pallas_call(
        functools.partial(block_kernel, scale, split),
        name="block_stage",
        grid_spec=pltpu.PrefetchScalarGridSpec(
            num_scalar_prefetch=1,
            grid=(count,),
            in_specs=[
                pl.BlockSpec((WIN, rows, expanded), lambda b, me: (b + start, 0, 0)),
                pl.BlockSpec((WIN, rows, channels), lambda b, me: (b + start, 0, 0)),
            ]
            + [whole(p.shape) for p in (parts, up, proj, *params)],
            out_specs=partner_specs(split, rows, channels),
            scratch_shapes=[
                pltpu.VMEM((8, expanded), F32),
                pltpu.VMEM((WIN, rows, channels), BF16),
            ]
            + attention_scratch(cells, channels),
        ),
        out_shape=partner_shapes(split, count, rows, channels),
        cost_estimate=pl.CostEstimate(
            flops=1_000_000,
            bytes_accessed=100_000,
            transcendentals=0,
        ),
        compiler_params=pltpu.CompilerParams(vmem_limit_bytes=VMEM_BYTES),
    )(me, active, field, parts, up, proj, *params)


def grid_stage(split_in, split_out, me, received, perm, params):
    count, rows, channels = received[0].shape[-3:]
    cells = WIN * rows
    return pl.pallas_call(
        functools.partial(grid_kernel, split_in, split_out),
        name="grid_stage",
        grid_spec=pltpu.PrefetchScalarGridSpec(
            num_scalar_prefetch=1,
            grid=(count,),
            in_specs=partner_specs(split_in, rows, channels)
            + [whole((cells, cells))]
            + [whole(p.shape) for p in params],
            out_specs=partner_specs(split_out, rows, channels),
            scratch_shapes=[pltpu.VMEM((WIN, rows, channels), BF16)]
            + attention_scratch(cells, channels),
        ),
        out_shape=partner_shapes(split_out, count, rows, channels),
        cost_estimate=pl.CostEstimate(
            flops=1_000_000,
            bytes_accessed=100_000,
            transcendentals=0,
        ),
        compiler_params=pltpu.CompilerParams(vmem_limit_bytes=VMEM_BYTES),
    )(me, *received, perm, *params)


def merge_stage(split, start, total, me, received, perm, merged):
    count, rows, channels = received[0].shape[-3:]
    cells = WIN * rows
    n = len(received)
    return pl.pallas_call(
        functools.partial(merge_kernel, split),
        name="merge_stage",
        grid_spec=pltpu.PrefetchScalarGridSpec(
            num_scalar_prefetch=1,
            grid=(count,),
            in_specs=partner_specs(split, rows, channels)
            + [whole((cells, cells))]
            + [pl.BlockSpec(memory_space=pl.ANY)] * (merged is not None),
            out_specs=pl.BlockSpec((rows, WIN, channels), lambda b, me: (0, b + start, 0)),
        ),
        out_shape=jax.ShapeDtypeStruct((rows, total * WIN, channels), BF16),
        input_output_aliases={} if merged is None else {n + 2: 0},
        cost_estimate=pl.CostEstimate(
            flops=1_000_000,
            bytes_accessed=100_000,
            transcendentals=0,
        ),
        compiler_params=pltpu.CompilerParams(vmem_limit_bytes=VMEM_BYTES),
    )(me, *received, perm, *([] if merged is None else [merged]))


def turned_bias(pos_table):
    position = jnp.arange(CELLS)
    row = position % WIN
    col = position // WIN
    index = (row[None, :] - row[:, None] + 7) * 15 + (col[None, :] - col[:, None] + 7)
    one_hot = (index[:, :, None] == jnp.arange(225)[None, None, :]).astype(F32)
    bias = jnp.einsum("jir,rh->jhi", one_hot, pos_table * LOG2E, precision=lax.Precision.HIGHEST)
    return bias.reshape(CELLS, HEADS * CELLS)


def attention_params(gain, in_weight, out_weight, pos_table):
    return gain.reshape(1, -1), in_weight, out_weight, turned_bias(pos_table)


def cell_orders(rows, place):
    per = rows // WIN
    cells = jnp.arange(WIN * rows)
    window, col, row = cells // CELLS, cells // WIN % WIN, cells % WIN
    into = (col ^ place) * rows + row * per + window
    row, col = cells // WIN, cells % WIN
    back = (col ^ place) * rows + row % per * WIN + row // per
    return tuple((source[:, None] == cells[None, :]).astype(BF16) for source in (into, back))


def per_device(
    input_field,
    expand_weight,
    expand_bias,
    depth_weight,
    depth_bias,
    squeeze_down,
    squeeze_up,
    project_weight,
    block_gain,
    block_in_weight,
    block_out_weight,
    block_table,
    grid_gain,
    grid_in_weight,
    grid_out_weight,
    grid_table,
):
    rows, cols, channels = input_field.shape
    count = lax.axis_size("lon")
    per = count // WIN
    groups = [[j * per + r for j in range(WIN)] for r in range(per)]
    total = cols // WIN
    chunks = CHUNKS if sum(c[0] for c in CHUNKS) == total else ((total, False, False),)
    place = lax.axis_index("lon") // per
    places = {True: place.reshape(1).astype(jnp.int32), False: jnp.zeros((1,), jnp.int32)}
    before = lax.ppermute(
        jnp.swapaxes(input_field[:, -1:], 0, 1),
        "lon",
        [(i, (i + 1) % count) for i in range(count)],
    )
    after = lax.ppermute(
        jnp.swapaxes(input_field[:, :1], 0, 1),
        "lon",
        [((i + 1) % count, i) for i in range(count)],
    )
    field = jnp.swapaxes(input_field, 0, 1)
    active, part = mbconv(
        count, field, before, after, expand_weight, expand_bias, depth_weight, depth_bias,
        squeeze_down,
    )
    parts = lax.all_to_all(part, "lon", 0, 0, tiled=True)
    scale = ROOT_HALF / (rows * cols * count)
    into, back = {}, {}
    for split in sorted({split for _, *both in chunks for split in both}):
        into[split], back[split] = cell_orders(rows, places[split][0])
    block_params = attention_params(block_gain, block_in_weight, block_out_weight, block_table)
    grid_params = attention_params(grid_gain, grid_in_weight, grid_out_weight, grid_table)

    def exchange(split, pieces):
        if not split:
            return [
                lax.all_to_all(
                    pieces[0], "lon", 0, 0, axis_index_groups=groups, tiled=True
                )
            ]
        return [pieces[0]] + [
            lax.ppermute(
                pieces[s],
                "lon",
                [(j * per + r, (j ^ s) * per + r) for j in range(WIN) for r in range(per)],
            )
            for s in range(1, WIN)
        ]

    starts = [sum(c[0] for c in chunks[:k]) for k in range(len(chunks))]
    sent = [
        block_stage(
            split, start, size, scale, places[split], active, field, parts, squeeze_up,
            project_weight, block_params,
        )
        for start, (size, split, _) in zip(starts, chunks)
    ]
    received = [exchange(split, pieces) for pieces, (_, split, _) in zip(sent, chunks)]
    results = []
    for k, (_, split, returned) in enumerate(chunks):
        pieces = received[k]
        if k + 1 < len(chunks):
            later = sent[k + 1][0]
            pieces, _ = lax.optimization_barrier((pieces, later))
        me = places[split or returned]
        results.append(grid_stage(split, returned, me, pieces, into[split], grid_params))
    merged = None
    for start, result, (_, _, split) in zip(starts, results, chunks):
        merged = merge_stage(
            split, start, total, places[split], exchange(split, result), back[split], merged
        )
    return merged


def solution(mesh):
    return jax.shard_map(
        per_device,
        mesh=mesh,
        in_specs=(P("groups", "lon", None),) + (P(),) * 15,
        out_specs=P("groups", "lon", None),
        check_vma=False,
    )
```

```python
import functools

import jax
import jax.numpy as jnp
import numpy as np
from jax import lax
from jax.experimental import pallas as pl
from jax.experimental.pallas import tpu as pltpu
from jax.sharding import PartitionSpec as P

HEADS = 16
HEAD_DIM = 32
WIN = 8
CELLS = WIN * WIN
CHUNKS = ((2, False, True), (2, False, True))
LANES = 512
SUB = 256
VMEM_BYTES = 60 << 20
ROOT_HALF = 0.7071067811865476
LOG2E = 1.4426950408889634
SCORE_SCALE = HEAD_DIM ** (-0.5) * LOG2E
BF16 = jnp.bfloat16
F32 = jnp.float32


def whole(shape):
    return pl.BlockSpec(shape, lambda *_: (0,) * len(shape), pipeline_mode=pl.Buffered(1))


def double_gelu(half):
    return half + half * lax.erf(half)


def mbconv_kernel(
    x_ref, before_ref, after_ref, w_ref, b_ref, dw_ref, db_ref, down_ref, shift_ref,
    act_ref, part_ref, total_ref, tap_ref, *hidden_refs,
):
    out_cols, rows, channels = x_ref.shape
    lanes = w_ref.shape[1]
    sub = hidden_refs[0].shape[2]
    half = out_cols // 2
    pieces = 2
    piece = half + 1
    shift = shift_ref[...]
    for k in range(9):
        tap_ref[k] = jnp.broadcast_to(dw_ref[k : k + 1] * 0.5, (16, lanes)).astype(BF16)

    def expand(s, i):
        span = slice(s * sub, (s + 1) * sub)
        if i == 0:
            cells = jnp.concatenate([before_ref[...], x_ref[:half]], axis=0)
        else:
            cells = jnp.concatenate([x_ref[half:], after_ref[...]], axis=0)
        cells = cells.reshape(piece * rows, channels)
        hidden = jnp.dot(cells, w_ref[:, span], preferred_element_type=F32)
        hidden = double_gelu(hidden * ROOT_HALF + b_ref[:, span] * ROOT_HALF)
        hidden_refs[s][i * piece : (i + 1) * piece] = hidden.astype(BF16).reshape(piece, rows, sub)

    def depth(s, c, total):
        span = slice(s * sub, (s + 1) * sub)
        near = [hidden_refs[s][c + k].reshape(rows // 16, 16, sub) for k in range(3)]
        sums = []
        for r in range(3):
            terms = [near[k] * tap_ref[3 * r + k, :, span][None] for k in range(3)]
            sums.append((terms[0] + terms[1] + terms[2]).reshape(rows, sub))
        summed = jnp.dot(shift, jnp.concatenate(sums, axis=0), preferred_element_type=F32)
        active = double_gelu(summed + db_ref[:, span] * ROOT_HALF)
        act_ref[c, :, span] = active.astype(BF16)
        return total + active.reshape(rows // 8, 8, sub).sum(0)

    for i in range(pieces):
        expand(0, i)
    for s in range(len(hidden_refs)):
        total = jnp.zeros((8, sub), F32)
        for i in range(pieces):
            if s + 1 < len(hidden_refs):
                expand(s + 1, i)
            for c in range(i * out_cols // pieces, (i + 1) * out_cols // pieces):
                total = depth(s, c, total)
        total_ref[:, s * sub : (s + 1) * sub] = total
    pooled = jnp.sum(total_ref[...], axis=0, keepdims=True)
    part = jnp.dot(
        jnp.broadcast_to(pooled, (8, lanes)),
        down_ref[...].astype(F32),
        precision=lax.Precision.HIGHEST,
        preferred_element_type=F32,
    )[None]

    @pl.when(pl.program_id(0) == 0)
    def _():
        part_ref[...] = jnp.broadcast_to(part, part_ref.shape)

    @pl.when(pl.program_id(0) > 0)
    def _():
        part_ref[...] += part


def row_shifts(rows):
    shift = np.zeros((rows, 3 * rows), np.float32)
    for offset in range(3):
        for row in range(rows):
            if 0 <= row + offset - 1 < rows:
                shift[row, offset * rows + row + offset - 1] = 1.0
    return jnp.asarray(shift, BF16)


def mbconv(
    count, field, before, after, expand_weight, expand_bias, depth_weight, depth_bias, squeeze_down
):
    cols, rows, channels = field.shape
    expanded = expand_weight.shape[1]
    squeeze = squeeze_down.shape[1]
    return pl.pallas_call(
        mbconv_kernel,
        name="mbconv",
        grid=(expanded // LANES,),
        in_specs=[
            whole(field.shape),
            whole(before.shape),
            whole(after.shape),
            pl.BlockSpec((channels, LANES), lambda i: (0, i)),
            pl.BlockSpec((1, LANES), lambda i: (0, i)),
            pl.BlockSpec((9, LANES), lambda i: (0, i)),
            pl.BlockSpec((1, LANES), lambda i: (0, i)),
            pl.BlockSpec((LANES, squeeze), lambda i: (i, 0)),
            pl.BlockSpec((rows, 3 * rows), lambda i: (0, 0)),
        ],
        out_specs=[
            pl.BlockSpec((cols, rows, LANES), lambda i: (0, 0, i)),
            pl.BlockSpec((count, 8, squeeze), lambda i: (0, 0, 0)),
        ],
        out_shape=[
            jax.ShapeDtypeStruct((cols, rows, expanded), BF16),
            jax.ShapeDtypeStruct((count, 8, squeeze), F32),
        ],
        scratch_shapes=[pltpu.VMEM((8, LANES), F32), pltpu.VMEM((9, 16, LANES), BF16)]
        + [pltpu.VMEM((cols + 2, rows, SUB), BF16)] * (LANES // SUB),
        cost_estimate=pl.CostEstimate(
            flops=2 * cols * rows * channels * expanded * 4,
            bytes_accessed=20_000_000,
            transcendentals=0,
        ),
        compiler_params=pltpu.CompilerParams(vmem_limit_bytes=VMEM_BYTES),
    )(
        field,
        before,
        after,
        expand_weight,
        expand_bias.reshape(1, -1),
        depth_weight,
        depth_bias.reshape(1, -1),
        squeeze_down,
        row_shifts(rows),
    )


def prepare(in_ref, wv_ref, mask_ref):
    channels = in_ref.shape[0]
    wv_ref[...] = in_ref[:, 2 * channels :].T
    head = lax.broadcasted_iota(jnp.int32, mask_ref.shape, 0) // CELLS
    lane = lax.broadcasted_iota(jnp.int32, mask_ref.shape, 1) // HEAD_DIM
    mask_ref[...] = (head == lane).astype(F32).astype(BF16)


def attend(stream, gain_ref, in_ref, out_weight_ref, bias_ref, scratch):
    wv_ref, mask_ref, q_ref, k_ref, vt_ref, o_ref = scratch
    cells, channels = stream.shape
    average = jnp.mean(stream, axis=-1, keepdims=True)
    centred = stream - average
    variance = jnp.mean(centred * centred, axis=-1, keepdims=True)
    normed = (centred * lax.rsqrt(variance + 1e-05) * gain_ref[...]).astype(BF16)
    q_ref[...] = jnp.dot(normed, in_ref[:, :channels], preferred_element_type=F32).astype(BF16)
    k_ref[...] = jnp.dot(
        normed, in_ref[:, channels : 2 * channels], preferred_element_type=F32
    ).astype(BF16)
    vt_ref[...] = lax.dot_general(
        wv_ref[...], normed, (((1,), (1,)), ((), ())), preferred_element_type=F32
    ).astype(BF16)
    group = 256 // HEAD_DIM
    even = (lax.broadcasted_iota(jnp.int32, (CELLS, 128), 1) // HEAD_DIM) % 2 == 0
    zero = jnp.zeros((CELLS, 128), BF16)
    for duo in range(cells // 128):
        both = slice(duo * 128, (duo + 1) * 128)
        for g in range(HEADS // group):
            part = slice(g * 256, (g + 1) * 256)
            lanes = slice(g * group * CELLS, (g + 1) * group * CELLS)
            probs = []
            for w in (2 * duo, 2 * duo + 1):
                span = slice(w * CELLS, (w + 1) * CELLS)
                query = jnp.concatenate([q_ref[span, part]] * group, axis=0) * mask_ref[...]
                scores = lax.dot_general(
                    k_ref[span, part], query, (((1,), (1,)), ((), ())), preferred_element_type=F32
                )
                scores = scores * SCORE_SCALE + bias_ref[:, lanes]
                scores = jnp.exp2(scores - jnp.max(scores, axis=0, keepdims=True))
                weight = 1.0 / jnp.sum(scores, axis=0, keepdims=True)
                probs.append((scores * weight).astype(BF16))
            for quad in range(group // 4):
                outs = []
                for pair in (2 * quad, 2 * quad + 1):
                    c = slice(pair * 128, (pair + 1) * 128)
                    right = jnp.concatenate(
                        [
                            jnp.concatenate([probs[0][:, c], zero], axis=1),
                            jnp.concatenate([zero, probs[1][:, c]], axis=1),
                        ],
                        axis=0,
                    )
                    first = g * 256 + pair * 64
                    outs.append(
                        jnp.dot(
                            vt_ref[first : first + 64, both], right, preferred_element_type=F32
                        )
                    )
                first = g * 256 + quad * 128
                for k in range(2):
                    turned = jnp.concatenate([o[:, k * 128 : (k + 1) * 128] for o in outs], axis=0)
                    turned = turned.T
                    picked = jnp.where(even, turned[:CELLS], turned[CELLS:])
                    row = (2 * duo + k) * CELLS
                    o_ref[row : row + CELLS, first : first + 128] = picked.astype(BF16)
    return stream + jnp.dot(o_ref[...], out_weight_ref[...], preferred_element_type=F32)


def block_kernel(
    scale, split, me_ref, act_ref, x_ref, part_ref, up_ref, proj_ref, gain_ref, in_ref,
    out_weight_ref, bias_ref, *refs,
):
    outs, (gate_ref, sent_ref, *scratch) = (refs[:WIN], refs[WIN:]) if split else (refs[:1], refs[1:])
    cols, rows, expanded = act_ref.shape
    channels = x_ref.shape[2]

    @pl.when(pl.program_id(0) == 0)
    def _():
        squeezed = jnp.sum(part_ref[...], axis=0) * scale
        squeezed = squeezed * jax.nn.sigmoid(squeezed)
        gate = jnp.dot(
            squeezed,
            up_ref[...].astype(F32),
            precision=lax.Precision.HIGHEST,
            preferred_element_type=F32,
        )
        gate_ref[...] = jax.nn.sigmoid(gate) * ROOT_HALF
        prepare(in_ref, scratch[0], scratch[1])

    gated = act_ref[...].reshape(cols * rows, expanded).astype(F32) * gate_ref[0:1]
    first = jnp.dot(gated.astype(BF16), proj_ref[...], preferred_element_type=F32)
    first = first.reshape(cols, rows, channels) + x_ref[...].astype(F32)
    first = first.astype(BF16).astype(F32)
    windows = rows // WIN
    stream = jnp.concatenate(
        [first[:, a * WIN : (a + 1) * WIN].reshape(CELLS, channels) for a in range(windows)],
        axis=0,
    )
    second = attend(stream, gain_ref, in_ref, out_weight_ref, bias_ref, scratch)
    second = second.reshape(windows, cols, WIN, channels)
    second = jnp.concatenate([second[a] for a in range(windows)], axis=1).astype(BF16)
    deliver(second, me_ref, outs, sent_ref)


def deliver(pieces, me_ref, outs, sent_ref):
    if len(outs) == 1:
        outs[0][:, 0] = pieces
        return
    sent_ref[...] = pieces
    for s in range(WIN):
        outs[s][0] = sent_ref[me_ref[0] ^ s]


def gathered(ins):
    if len(ins) == 1:
        return ins[0][...].reshape(-1, ins[0].shape[-1])
    return jnp.concatenate([ref[0] for ref in ins], axis=0)


def grid_kernel(split_in, split_out, me_ref, *refs):
    n = WIN if split_in else 1
    ins, refs = refs[:n], refs[n:]
    perm_ref, gain_ref, in_ref, out_weight_ref, bias_ref = refs[:5]
    n = WIN if split_out else 1
    outs, (sent_ref, *scratch) = refs[5 : 5 + n], refs[5 + n :]

    @pl.when(pl.program_id(0) == 0)
    def _():
        prepare(in_ref, scratch[0], scratch[1])

    stream = jnp.dot(perm_ref[...], gathered(ins), preferred_element_type=F32)
    result = attend(stream, gain_ref, in_ref, out_weight_ref, bias_ref, scratch)
    channels = result.shape[1]
    result = result.reshape(-1, WIN, WIN, channels)
    result = jnp.concatenate([result[a] for a in range(result.shape[0])], axis=1).astype(BF16)
    deliver(result, me_ref, outs, sent_ref)


def merge_kernel(split, me_ref, *refs):
    n = WIN if split else 1
    ins, perm_ref, out_ref = refs[:n], refs[n], refs[-1]
    cells = jnp.dot(perm_ref[...], gathered(ins), preferred_element_type=F32)
    out_ref[...] = cells.reshape(out_ref.shape).astype(BF16)


def attention_scratch(cells, channels):
    return [
        pltpu.VMEM((channels, channels), BF16),
        pltpu.VMEM((256 // HEAD_DIM * CELLS, 256), BF16),
        pltpu.VMEM((cells, channels), BF16),
        pltpu.VMEM((cells, channels), BF16),
        pltpu.VMEM((channels, cells), BF16),
        pltpu.VMEM((cells, channels), BF16),
    ]


def partner_specs(split, rows, channels):
    if split:
        return [pl.BlockSpec((1, rows, channels), lambda b, me: (b, 0, 0))] * WIN
    return [pl.BlockSpec((WIN, 1, rows, channels), lambda b, me: (0, b, 0, 0))]


def partner_shapes(split, count, rows, channels):
    if split:
        return [jax.ShapeDtypeStruct((count, rows, channels), BF16)] * WIN
    return [jax.ShapeDtypeStruct((WIN, count, rows, channels), BF16)]


def block_stage(split, start, count, scale, me, active, field, parts, up, proj, params):
    cols, rows, channels = field.shape
    expanded = active.shape[2]
    cells = WIN * rows
    return pl.pallas_call(
        functools.partial(block_kernel, scale, split),
        name="block_stage",
        grid_spec=pltpu.PrefetchScalarGridSpec(
            num_scalar_prefetch=1,
            grid=(count,),
            in_specs=[
                pl.BlockSpec((WIN, rows, expanded), lambda b, me: (b + start, 0, 0)),
                pl.BlockSpec((WIN, rows, channels), lambda b, me: (b + start, 0, 0)),
            ]
            + [whole(p.shape) for p in (parts, up, proj, *params)],
            out_specs=partner_specs(split, rows, channels),
            scratch_shapes=[
                pltpu.VMEM((8, expanded), F32),
                pltpu.VMEM((WIN, rows, channels), BF16),
            ]
            + attention_scratch(cells, channels),
        ),
        out_shape=partner_shapes(split, count, rows, channels),
        cost_estimate=pl.CostEstimate(
            flops=1_000_000,
            bytes_accessed=100_000,
            transcendentals=0,
        ),
        compiler_params=pltpu.CompilerParams(vmem_limit_bytes=VMEM_BYTES),
    )(me, active, field, parts, up, proj, *params)


def grid_stage(split_in, split_out, me, received, perm, params):
    count, rows, channels = received[0].shape[-3:]
    cells = WIN * rows
    return pl.pallas_call(
        functools.partial(grid_kernel, split_in, split_out),
        name="grid_stage",
        grid_spec=pltpu.PrefetchScalarGridSpec(
            num_scalar_prefetch=1,
            grid=(count,),
            in_specs=partner_specs(split_in, rows, channels)
            + [whole((cells, cells))]
            + [whole(p.shape) for p in params],
            out_specs=partner_specs(split_out, rows, channels),
            scratch_shapes=[pltpu.VMEM((WIN, rows, channels), BF16)]
            + attention_scratch(cells, channels),
        ),
        out_shape=partner_shapes(split_out, count, rows, channels),
        cost_estimate=pl.CostEstimate(
            flops=1_000_000,
            bytes_accessed=100_000,
            transcendentals=0,
        ),
        compiler_params=pltpu.CompilerParams(vmem_limit_bytes=VMEM_BYTES),
    )(me, *received, perm, *params)


def merge_stage(split, start, total, me, received, perm, merged):
    count, rows, channels = received[0].shape[-3:]
    cells = WIN * rows
    n = len(received)
    return pl.pallas_call(
        functools.partial(merge_kernel, split),
        name="merge_stage",
        grid_spec=pltpu.PrefetchScalarGridSpec(
            num_scalar_prefetch=1,
            grid=(count,),
            in_specs=partner_specs(split, rows, channels)
            + [whole((cells, cells))]
            + [pl.BlockSpec(memory_space=pl.ANY)] * (merged is not None),
            out_specs=pl.BlockSpec((rows, WIN, channels), lambda b, me: (0, b + start, 0)),
        ),
        out_shape=jax.ShapeDtypeStruct((rows, total * WIN, channels), BF16),
        input_output_aliases={} if merged is None else {n + 2: 0},
        cost_estimate=pl.CostEstimate(
            flops=1_000_000,
            bytes_accessed=100_000,
            transcendentals=0,
        ),
        compiler_params=pltpu.CompilerParams(vmem_limit_bytes=VMEM_BYTES),
    )(me, *received, perm, *([] if merged is None else [merged]))


def turned_bias(pos_table):
    position = jnp.arange(CELLS)
    row = position % WIN
    col = position // WIN
    index = (row[None, :] - row[:, None] + 7) * 15 + (col[None, :] - col[:, None] + 7)
    one_hot = (index[:, :, None] == jnp.arange(225)[None, None, :]).astype(F32)
    bias = jnp.einsum("jir,rh->jhi", one_hot, pos_table * LOG2E, precision=lax.Precision.HIGHEST)
    return bias.reshape(CELLS, HEADS * CELLS)


def attention_params(gain, in_weight, out_weight, pos_table):
    return gain.reshape(1, -1), in_weight, out_weight, turned_bias(pos_table)


def cell_orders(rows, place):
    per = rows // WIN
    cells = jnp.arange(WIN * rows)
    window, col, row = cells // CELLS, cells // WIN % WIN, cells % WIN
    into = (col ^ place) * rows + row * per + window
    row, col = cells // WIN, cells % WIN
    back = (col ^ place) * rows + row % per * WIN + row // per
    return tuple((source[:, None] == cells[None, :]).astype(BF16) for source in (into, back))


def per_device(
    input_field,
    expand_weight,
    expand_bias,
    depth_weight,
    depth_bias,
    squeeze_down,
    squeeze_up,
    project_weight,
    block_gain,
    block_in_weight,
    block_out_weight,
    block_table,
    grid_gain,
    grid_in_weight,
    grid_out_weight,
    grid_table,
):
    rows, cols, channels = input_field.shape
    count = lax.axis_size("lon")
    per = count // WIN
    groups = [[j * per + r for j in range(WIN)] for r in range(per)]
    total = cols // WIN
    chunks = CHUNKS if sum(c[0] for c in CHUNKS) == total else ((total, False, False),)
    place = lax.axis_index("lon") // per
    places = {True: place.reshape(1).astype(jnp.int32), False: jnp.zeros((1,), jnp.int32)}
    edges = lax.optimization_barrier(input_field)
    before = lax.ppermute(
        jnp.swapaxes(edges[:, -1:], 0, 1),
        "lon",
        [(i, (i + 1) % count) for i in range(count)],
    )
    after = lax.ppermute(
        jnp.swapaxes(edges[:, :1], 0, 1),
        "lon",
        [((i + 1) % count, i) for i in range(count)],
    )
    field = jnp.swapaxes(input_field, 0, 1)
    active, part = mbconv(
        count, field, before, after, expand_weight, expand_bias, depth_weight, depth_bias,
        squeeze_down,
    )
    parts = lax.all_to_all(part, "lon", 0, 0, tiled=True)
    scale = ROOT_HALF / (rows * cols * count)
    into, back = {}, {}
    for split in sorted({split for _, *both in chunks for split in both}):
        into[split], back[split] = cell_orders(rows, places[split][0])
    block_params = attention_params(block_gain, block_in_weight, block_out_weight, block_table)
    grid_params = attention_params(grid_gain, grid_in_weight, grid_out_weight, grid_table)

    def exchange(split, pieces):
        if not split:
            return [
                lax.all_to_all(
                    pieces[0], "lon", 0, 0, axis_index_groups=groups, tiled=True
                )
            ]
        return [pieces[0]] + [
            lax.ppermute(
                pieces[s],
                "lon",
                [(j * per + r, (j ^ s) * per + r) for j in range(WIN) for r in range(per)],
            )
            for s in range(1, WIN)
        ]

    starts = [sum(c[0] for c in chunks[:k]) for k in range(len(chunks))]
    sent = [
        block_stage(
            split, start, size, scale, places[split], active, field, parts, squeeze_up,
            project_weight, block_params,
        )
        for start, (size, split, _) in zip(starts, chunks)
    ]
    if len(chunks) > 1:
        sent[1], grid_params, into, back = lax.optimization_barrier(
            (sent[1], grid_params, into, back)
        )
    received = [exchange(split, pieces) for pieces, (_, split, _) in zip(sent, chunks)]
    results = []
    for k, (_, split, returned) in enumerate(chunks):
        pieces = received[k]
        if k + 1 < len(chunks):
            later = sent[k + 1][0]
            pieces, _ = lax.optimization_barrier((pieces, later))
        me = places[split or returned]
        results.append(grid_stage(split, returned, me, pieces, into[split], grid_params))
    merged = None
    for start, result, (_, _, split) in zip(starts, results, chunks):
        merged = merge_stage(
            split, start, total, places[split], exchange(split, result), back[split], merged
        )
    return merged


def solution(mesh):
    return jax.shard_map(
        per_device,
        mesh=mesh,
        in_specs=(P("groups", "lon", None),) + (P(),) * 15,
        out_specs=P("groups", "lon", None),
        check_vma=False,
    )
```

```python
import functools

import jax
import jax.numpy as jnp
import numpy as np
from jax import lax
from jax.experimental import pallas as pl
from jax.experimental.pallas import tpu as pltpu
from jax.sharding import PartitionSpec as P

HEADS = 16
HEAD_DIM = 32
WIN = 8
CELLS = WIN * WIN
CHUNKS = ((2, False, True), (2, False, True))
TIED = 4
LANES = 512
SUB = 256
VMEM_BYTES = 60 << 20
ROOT_HALF = 0.7071067811865476
LOG2E = 1.4426950408889634
SCORE_SCALE = HEAD_DIM ** (-0.5) * LOG2E
BF16 = jnp.bfloat16
F32 = jnp.float32


def whole(shape):
    return pl.BlockSpec(shape, lambda *_: (0,) * len(shape), pipeline_mode=pl.Buffered(1))


def double_gelu(half):
    return half + half * lax.erf(half)


def mbconv_kernel(
    x_ref, before_ref, after_ref, w_ref, b_ref, dw_ref, db_ref, down_ref, shift_ref,
    act_ref, part_ref, total_ref, tap_ref, *hidden_refs,
):
    out_cols, rows, channels = x_ref.shape
    lanes = w_ref.shape[1]
    sub = hidden_refs[0].shape[2]
    half = out_cols // 2
    pieces = 2
    piece = half + 1
    shift = shift_ref[...]
    for k in range(9):
        tap_ref[k] = jnp.broadcast_to(dw_ref[k : k + 1] * 0.5, (16, lanes)).astype(BF16)

    def expand(s, i):
        span = slice(s * sub, (s + 1) * sub)
        if i == 0:
            cells = jnp.concatenate([before_ref[...], x_ref[:half]], axis=0)
        else:
            cells = jnp.concatenate([x_ref[half:], after_ref[...]], axis=0)
        cells = cells.reshape(piece * rows, channels)
        hidden = jnp.dot(cells, w_ref[:, span], preferred_element_type=F32)
        hidden = double_gelu(hidden * ROOT_HALF + b_ref[:, span] * ROOT_HALF)
        hidden_refs[s][i * piece : (i + 1) * piece] = hidden.astype(BF16).reshape(piece, rows, sub)

    def depth(s, c, total):
        span = slice(s * sub, (s + 1) * sub)
        near = [hidden_refs[s][c + k].reshape(rows // 16, 16, sub) for k in range(3)]
        sums = []
        for r in range(3):
            terms = [near[k] * tap_ref[3 * r + k, :, span][None] for k in range(3)]
            sums.append((terms[0] + terms[1] + terms[2]).reshape(rows, sub))
        summed = jnp.dot(shift, jnp.concatenate(sums, axis=0), preferred_element_type=F32)
        active = double_gelu(summed + db_ref[:, span] * ROOT_HALF)
        act_ref[c, :, span] = active.astype(BF16)
        return total + active.reshape(rows // 8, 8, sub).sum(0)

    for i in range(pieces):
        expand(0, i)
    for s in range(len(hidden_refs)):
        total = jnp.zeros((8, sub), F32)
        for i in range(pieces):
            if s + 1 < len(hidden_refs):
                expand(s + 1, i)
            for c in range(i * out_cols // pieces, (i + 1) * out_cols // pieces):
                total = depth(s, c, total)
        total_ref[:, s * sub : (s + 1) * sub] = total
    pooled = jnp.sum(total_ref[...], axis=0, keepdims=True)
    part = jnp.dot(
        jnp.broadcast_to(pooled, (8, lanes)),
        down_ref[...].astype(F32),
        precision=lax.Precision.HIGHEST,
        preferred_element_type=F32,
    )[None]

    @pl.when(pl.program_id(0) == 0)
    def _():
        part_ref[...] = jnp.broadcast_to(part, part_ref.shape)

    @pl.when(pl.program_id(0) > 0)
    def _():
        part_ref[...] += part


def row_shifts(rows):
    shift = np.zeros((rows, 3 * rows), np.float32)
    for offset in range(3):
        for row in range(rows):
            if 0 <= row + offset - 1 < rows:
                shift[row, offset * rows + row + offset - 1] = 1.0
    return jnp.asarray(shift, BF16)


def mbconv(
    count, field, before, after, expand_weight, expand_bias, depth_weight, depth_bias, squeeze_down
):
    cols, rows, channels = field.shape
    expanded = expand_weight.shape[1]
    squeeze = squeeze_down.shape[1]
    return pl.pallas_call(
        mbconv_kernel,
        name="mbconv",
        grid=(expanded // LANES,),
        in_specs=[
            whole(field.shape),
            whole(before.shape),
            whole(after.shape),
            pl.BlockSpec((channels, LANES), lambda i: (0, i)),
            pl.BlockSpec((1, LANES), lambda i: (0, i)),
            pl.BlockSpec((9, LANES), lambda i: (0, i)),
            pl.BlockSpec((1, LANES), lambda i: (0, i)),
            pl.BlockSpec((LANES, squeeze), lambda i: (i, 0)),
            pl.BlockSpec((rows, 3 * rows), lambda i: (0, 0)),
        ],
        out_specs=[
            pl.BlockSpec((cols, rows, LANES), lambda i: (0, 0, i)),
            pl.BlockSpec((count, 8, squeeze), lambda i: (0, 0, 0)),
        ],
        out_shape=[
            jax.ShapeDtypeStruct((cols, rows, expanded), BF16),
            jax.ShapeDtypeStruct((count, 8, squeeze), F32),
        ],
        scratch_shapes=[pltpu.VMEM((8, LANES), F32), pltpu.VMEM((9, 16, LANES), BF16)]
        + [pltpu.VMEM((cols + 2, rows, SUB), BF16)] * (LANES // SUB),
        cost_estimate=pl.CostEstimate(
            flops=2 * cols * rows * channels * expanded * 4,
            bytes_accessed=20_000_000,
            transcendentals=0,
        ),
        compiler_params=pltpu.CompilerParams(vmem_limit_bytes=VMEM_BYTES),
    )(
        field,
        before,
        after,
        expand_weight,
        expand_bias.reshape(1, -1),
        depth_weight,
        depth_bias.reshape(1, -1),
        squeeze_down,
        row_shifts(rows),
    )


def prepare(in_ref, wv_ref, mask_ref):
    channels = in_ref.shape[0]
    wv_ref[...] = in_ref[:, 2 * channels :].T
    head = lax.broadcasted_iota(jnp.int32, mask_ref.shape, 0) // CELLS
    lane = lax.broadcasted_iota(jnp.int32, mask_ref.shape, 1) // HEAD_DIM
    mask_ref[...] = (head == lane).astype(F32).astype(BF16)


def attend(stream, gain_ref, in_ref, out_weight_ref, bias_ref, scratch):
    wv_ref, mask_ref, q_ref, k_ref, vt_ref, o_ref = scratch
    cells, channels = stream.shape
    average = jnp.mean(stream, axis=-1, keepdims=True)
    centred = stream - average
    variance = jnp.mean(centred * centred, axis=-1, keepdims=True)
    normed = (centred * lax.rsqrt(variance + 1e-05) * gain_ref[...]).astype(BF16)
    q_ref[...] = jnp.dot(normed, in_ref[:, :channels], preferred_element_type=F32).astype(BF16)
    k_ref[...] = jnp.dot(
        normed, in_ref[:, channels : 2 * channels], preferred_element_type=F32
    ).astype(BF16)
    vt_ref[...] = lax.dot_general(
        wv_ref[...], normed, (((1,), (1,)), ((), ())), preferred_element_type=F32
    ).astype(BF16)
    group = 256 // HEAD_DIM
    even = (lax.broadcasted_iota(jnp.int32, (CELLS, 128), 1) // HEAD_DIM) % 2 == 0
    zero = jnp.zeros((CELLS, 128), BF16)
    for duo in range(cells // 128):
        both = slice(duo * 128, (duo + 1) * 128)
        for g in range(HEADS // group):
            part = slice(g * 256, (g + 1) * 256)
            lanes = slice(g * group * CELLS, (g + 1) * group * CELLS)
            probs = []
            for w in (2 * duo, 2 * duo + 1):
                span = slice(w * CELLS, (w + 1) * CELLS)
                query = jnp.concatenate([q_ref[span, part]] * group, axis=0) * mask_ref[...]
                scores = lax.dot_general(
                    k_ref[span, part], query, (((1,), (1,)), ((), ())), preferred_element_type=F32
                )
                scores = scores * SCORE_SCALE + bias_ref[:, lanes]
                scores = jnp.exp2(scores - jnp.max(scores, axis=0, keepdims=True))
                weight = 1.0 / jnp.sum(scores, axis=0, keepdims=True)
                probs.append((scores * weight).astype(BF16))
            for quad in range(group // 4):
                outs = []
                for pair in (2 * quad, 2 * quad + 1):
                    c = slice(pair * 128, (pair + 1) * 128)
                    right = jnp.concatenate(
                        [
                            jnp.concatenate([probs[0][:, c], zero], axis=1),
                            jnp.concatenate([zero, probs[1][:, c]], axis=1),
                        ],
                        axis=0,
                    )
                    first = g * 256 + pair * 64
                    outs.append(
                        jnp.dot(
                            vt_ref[first : first + 64, both], right, preferred_element_type=F32
                        )
                    )
                first = g * 256 + quad * 128
                for k in range(2):
                    turned = jnp.concatenate([o[:, k * 128 : (k + 1) * 128] for o in outs], axis=0)
                    turned = turned.T
                    picked = jnp.where(even, turned[:CELLS], turned[CELLS:])
                    row = (2 * duo + k) * CELLS
                    o_ref[row : row + CELLS, first : first + 128] = picked.astype(BF16)
    return stream + jnp.dot(o_ref[...], out_weight_ref[...], preferred_element_type=F32)


def block_kernel(
    scale, split, me_ref, act_ref, x_ref, part_ref, up_ref, proj_ref, gain_ref, in_ref,
    out_weight_ref, bias_ref, *refs,
):
    outs, (gate_ref, sent_ref, *scratch) = (refs[:WIN], refs[WIN:]) if split else (refs[:1], refs[1:])
    cols, rows, expanded = act_ref.shape
    channels = x_ref.shape[2]

    @pl.when(pl.program_id(0) == 0)
    def _():
        squeezed = jnp.sum(part_ref[...], axis=0) * scale
        squeezed = squeezed * jax.nn.sigmoid(squeezed)
        gate = jnp.dot(
            squeezed,
            up_ref[...].astype(F32),
            precision=lax.Precision.HIGHEST,
            preferred_element_type=F32,
        )
        gate_ref[...] = jax.nn.sigmoid(gate) * ROOT_HALF
        prepare(in_ref, scratch[0], scratch[1])

    gated = act_ref[...].reshape(cols * rows, expanded).astype(F32) * gate_ref[0:1]
    first = jnp.dot(gated.astype(BF16), proj_ref[...], preferred_element_type=F32)
    first = first.reshape(cols, rows, channels) + x_ref[...].astype(F32)
    first = first.astype(BF16).astype(F32)
    windows = rows // WIN
    stream = jnp.concatenate(
        [first[:, a * WIN : (a + 1) * WIN].reshape(CELLS, channels) for a in range(windows)],
        axis=0,
    )
    second = attend(stream, gain_ref, in_ref, out_weight_ref, bias_ref, scratch)
    second = second.reshape(windows, cols, WIN, channels)
    second = jnp.concatenate([second[a] for a in range(windows)], axis=1).astype(BF16)
    deliver(second, me_ref, outs, sent_ref)


def deliver(pieces, me_ref, outs, sent_ref):
    if len(outs) == 1:
        outs[0][:, 0] = pieces
        return
    sent_ref[...] = pieces
    for s in range(WIN):
        outs[s][0] = sent_ref[me_ref[0] ^ s]


def gathered(ins):
    if len(ins) == 1:
        return ins[0][...].reshape(-1, ins[0].shape[-1])
    return jnp.concatenate([ref[0] for ref in ins], axis=0)


def grid_kernel(split_in, split_out, me_ref, *refs):
    n = WIN if split_in else 1
    ins, refs = refs[:n], refs[n:]
    perm_ref, gain_ref, in_ref, out_weight_ref, bias_ref = refs[:5]
    n = WIN if split_out else 1
    outs, (sent_ref, *scratch) = refs[5 : 5 + n], refs[5 + n :]

    @pl.when(pl.program_id(0) == 0)
    def _():
        prepare(in_ref, scratch[0], scratch[1])

    stream = jnp.dot(perm_ref[...], gathered(ins), preferred_element_type=F32)
    result = attend(stream, gain_ref, in_ref, out_weight_ref, bias_ref, scratch)
    channels = result.shape[1]
    result = result.reshape(-1, WIN, WIN, channels)
    result = jnp.concatenate([result[a] for a in range(result.shape[0])], axis=1).astype(BF16)
    deliver(result, me_ref, outs, sent_ref)


def merge_kernel(split, me_ref, *refs):
    n = WIN if split else 1
    ins, perm_ref, out_ref = refs[:n], refs[n], refs[-1]
    cells = jnp.dot(perm_ref[...], gathered(ins), preferred_element_type=F32)
    out_ref[...] = cells.reshape(out_ref.shape).astype(BF16)


def attention_scratch(cells, channels):
    return [
        pltpu.VMEM((channels, channels), BF16),
        pltpu.VMEM((256 // HEAD_DIM * CELLS, 256), BF16),
        pltpu.VMEM((cells, channels), BF16),
        pltpu.VMEM((cells, channels), BF16),
        pltpu.VMEM((channels, cells), BF16),
        pltpu.VMEM((cells, channels), BF16),
    ]


def partner_specs(split, rows, channels):
    if split:
        return [pl.BlockSpec((1, rows, channels), lambda b, me: (b, 0, 0))] * WIN
    return [pl.BlockSpec((WIN, 1, rows, channels), lambda b, me: (0, b, 0, 0))]


def partner_shapes(split, count, rows, channels):
    if split:
        return [jax.ShapeDtypeStruct((count, rows, channels), BF16)] * WIN
    return [jax.ShapeDtypeStruct((WIN, count, rows, channels), BF16)]


def block_stage(split, start, count, scale, me, active, field, parts, up, proj, params):
    cols, rows, channels = field.shape
    expanded = active.shape[2]
    cells = WIN * rows
    return pl.pallas_call(
        functools.partial(block_kernel, scale, split),
        name="block_stage",
        grid_spec=pltpu.PrefetchScalarGridSpec(
            num_scalar_prefetch=1,
            grid=(count,),
            in_specs=[
                pl.BlockSpec((WIN, rows, expanded), lambda b, me: (b + start, 0, 0)),
                pl.BlockSpec((WIN, rows, channels), lambda b, me: (b + start, 0, 0)),
            ]
            + [whole(p.shape) for p in (parts, up, proj, *params)],
            out_specs=partner_specs(split, rows, channels),
            scratch_shapes=[
                pltpu.VMEM((8, expanded), F32),
                pltpu.VMEM((WIN, rows, channels), BF16),
            ]
            + attention_scratch(cells, channels),
        ),
        out_shape=partner_shapes(split, count, rows, channels),
        cost_estimate=pl.CostEstimate(
            flops=1_000_000,
            bytes_accessed=100_000,
            transcendentals=0,
        ),
        compiler_params=pltpu.CompilerParams(vmem_limit_bytes=VMEM_BYTES),
    )(me, active, field, parts, up, proj, *params)


def grid_stage(split_in, split_out, me, received, perm, params):
    count, rows, channels = received[0].shape[-3:]
    cells = WIN * rows
    return pl.pallas_call(
        functools.partial(grid_kernel, split_in, split_out),
        name="grid_stage",
        grid_spec=pltpu.PrefetchScalarGridSpec(
            num_scalar_prefetch=1,
            grid=(count,),
            in_specs=partner_specs(split_in, rows, channels)
            + [whole((cells, cells))]
            + [whole(p.shape) for p in params],
            out_specs=partner_specs(split_out, rows, channels),
            scratch_shapes=[pltpu.VMEM((WIN, rows, channels), BF16)]
            + attention_scratch(cells, channels),
        ),
        out_shape=partner_shapes(split_out, count, rows, channels),
        cost_estimate=pl.CostEstimate(
            flops=1_000_000,
            bytes_accessed=100_000,
            transcendentals=0,
        ),
        compiler_params=pltpu.CompilerParams(vmem_limit_bytes=VMEM_BYTES),
    )(me, *received, perm, *params)


def merge_stage(split, start, total, me, received, perm, merged):
    count, rows, channels = received[0].shape[-3:]
    cells = WIN * rows
    n = len(received)
    return pl.pallas_call(
        functools.partial(merge_kernel, split),
        name="merge_stage",
        grid_spec=pltpu.PrefetchScalarGridSpec(
            num_scalar_prefetch=1,
            grid=(count,),
            in_specs=partner_specs(split, rows, channels)
            + [whole((cells, cells))]
            + [pl.BlockSpec(memory_space=pl.ANY)] * (merged is not None),
            out_specs=pl.BlockSpec((rows, WIN, channels), lambda b, me: (0, b + start, 0)),
        ),
        out_shape=jax.ShapeDtypeStruct((rows, total * WIN, channels), BF16),
        input_output_aliases={} if merged is None else {n + 2: 0},
        cost_estimate=pl.CostEstimate(
            flops=1_000_000,
            bytes_accessed=100_000,
            transcendentals=0,
        ),
        compiler_params=pltpu.CompilerParams(vmem_limit_bytes=VMEM_BYTES),
    )(me, *received, perm, *([] if merged is None else [merged]))


def turned_bias(pos_table):
    position = jnp.arange(CELLS)
    row = position % WIN
    col = position // WIN
    index = (row[None, :] - row[:, None] + 7) * 15 + (col[None, :] - col[:, None] + 7)
    one_hot = (index[:, :, None] == jnp.arange(225)[None, None, :]).astype(F32)
    bias = jnp.einsum("jir,rh->jhi", one_hot, pos_table * LOG2E, precision=lax.Precision.HIGHEST)
    return bias.reshape(CELLS, HEADS * CELLS)


def attention_params(gain, in_weight, out_weight, pos_table):
    return gain.reshape(1, -1), in_weight, out_weight, turned_bias(pos_table)


def cell_orders(rows, place):
    per = rows // WIN
    cells = jnp.arange(WIN * rows)
    window, col, row = cells // CELLS, cells // WIN % WIN, cells % WIN
    into = (col ^ place) * rows + row * per + window
    row, col = cells // WIN, cells % WIN
    back = (col ^ place) * rows + row % per * WIN + row // per
    return tuple((source[:, None] == cells[None, :]).astype(BF16) for source in (into, back))


def per_device(
    input_field,
    expand_weight,
    expand_bias,
    depth_weight,
    depth_bias,
    squeeze_down,
    squeeze_up,
    project_weight,
    block_gain,
    block_in_weight,
    block_out_weight,
    block_table,
    grid_gain,
    grid_in_weight,
    grid_out_weight,
    grid_table,
):
    rows, cols, channels = input_field.shape
    count = lax.axis_size("lon")
    per = count // WIN
    groups = [[j * per + r for j in range(WIN)] for r in range(per)]
    total = cols // WIN
    chunks = CHUNKS if sum(c[0] for c in CHUNKS) == total else ((total, False, False),)
    place = lax.axis_index("lon") // per
    places = {True: place.reshape(1).astype(jnp.int32), False: jnp.zeros((1,), jnp.int32)}
    edges = lax.optimization_barrier(input_field)
    before = lax.ppermute(
        jnp.swapaxes(edges[:, -1:], 0, 1),
        "lon",
        [(i, (i + 1) % count) for i in range(count)],
    )
    after = lax.ppermute(
        jnp.swapaxes(edges[:, :1], 0, 1),
        "lon",
        [((i + 1) % count, i) for i in range(count)],
    )
    field = jnp.swapaxes(input_field, 0, 1)
    active, part = mbconv(
        count, field, before, after, expand_weight, expand_bias, depth_weight, depth_bias,
        squeeze_down,
    )
    parts = lax.all_to_all(part, "lon", 0, 0, tiled=True)
    scale = ROOT_HALF / (rows * cols * count)
    into, back = {}, {}
    for split in sorted({split for _, *both in chunks for split in both}):
        into[split], back[split] = cell_orders(rows, places[split][0])
    block_params = attention_params(block_gain, block_in_weight, block_out_weight, block_table)
    grid_params = attention_params(grid_gain, grid_in_weight, grid_out_weight, grid_table)

    def exchange(split, pieces):
        if not split:
            return [
                lax.all_to_all(
                    pieces[0], "lon", 0, 0, axis_index_groups=groups, tiled=True
                )
            ]
        return [pieces[0]] + [
            lax.ppermute(
                pieces[s],
                "lon",
                [(j * per + r, (j ^ s) * per + r) for j in range(WIN) for r in range(per)],
            )
            for s in range(1, WIN)
        ]

    starts = [sum(c[0] for c in chunks[:k]) for k in range(len(chunks))]
    sent = [
        block_stage(
            split, start, size, scale, places[split], active, field, parts, squeeze_up,
            project_weight, block_params,
        )
        for start, (size, split, _) in zip(starts, chunks)
    ]
    if len(chunks) > 1:
        sent[1], grid_params, into, back = lax.optimization_barrier(
            (sent[1], grid_params, into, back)
        )
    received = [exchange(split, pieces) for pieces, (_, split, _) in zip(sent, chunks)]
    results = []
    for k, (_, split, returned) in enumerate(chunks):
        pieces = received[k]
        if k + 1 < len(chunks):
            pieces, _ = lax.optimization_barrier((pieces, sent[k + 1][0]))
        if k > 0 and chunks[k - 1][2]:
            pieces, _ = lax.optimization_barrier((pieces, results[k - 1][1:TIED]))
        me = places[split or returned]
        result = grid_stage(split, returned, me, pieces, into[split], grid_params)
        results.append(exchange(returned, result))
    merged = None
    for start, result, (_, _, split) in zip(starts, results, chunks):
        merged = merge_stage(
            split, start, total, places[split], result, back[split], merged
        )
    return merged


def solution(mesh):
    return jax.shard_map(
        per_device,
        mesh=mesh,
        in_specs=(P("groups", "lon", None),) + (P(),) * 15,
        out_specs=P("groups", "lon", None),
        check_vma=False,
    )
```

```python
import functools

import jax
import jax.numpy as jnp
import numpy as np
from jax import lax
from jax.experimental import pallas as pl
from jax.experimental.pallas import tpu as pltpu
from jax.sharding import PartitionSpec as P

HEADS = 16
HEAD_DIM = 32
WIN = 8
CELLS = WIN * WIN
CHUNKS = ((2, False, True), (2, False, True))
TIED = 4
LANES = 512
SUB = 256
VMEM_BYTES = 60 << 20
ROOT_HALF = 0.7071067811865476
LOG2E = 1.4426950408889634
SCORE_SCALE = HEAD_DIM ** (-0.5) * LOG2E
BF16 = jnp.bfloat16
F32 = jnp.float32


def whole(shape):
    return pl.BlockSpec(shape, lambda *_: (0,) * len(shape), pipeline_mode=pl.Buffered(1))


def double_gelu(half):
    return half + half * lax.erf(half)


def exact_dot(values, weight):
    count = values.shape[0]
    high = values.astype(BF16).astype(F32)
    middle = (values - high).astype(BF16).astype(F32)
    parts = jnp.concatenate([high, middle, values - high - middle], axis=0).astype(BF16)
    sums = jnp.dot(parts, weight, preferred_element_type=F32)
    return sums[:count] + sums[count : 2 * count] + sums[2 * count :]


def mbconv_kernel(
    x_ref, before_ref, after_ref, w_ref, b_ref, dw_ref, db_ref, down_ref, shift_ref,
    act_ref, part_ref, total_ref, tap_ref, *hidden_refs,
):
    out_cols, rows, channels = x_ref.shape
    lanes = w_ref.shape[1]
    sub = hidden_refs[0].shape[2]
    half = out_cols // 2
    pieces = 2
    piece = half + 1
    shift = shift_ref[...]
    for k in range(9):
        tap_ref[k] = jnp.broadcast_to(dw_ref[k : k + 1] * 0.5, (16, lanes)).astype(BF16)

    def expand(s, i):
        span = slice(s * sub, (s + 1) * sub)
        if i == 0:
            cells = jnp.concatenate([before_ref[...], x_ref[:half]], axis=0)
        else:
            cells = jnp.concatenate([x_ref[half:], after_ref[...]], axis=0)
        cells = cells.reshape(piece * rows, channels)
        hidden = jnp.dot(cells, w_ref[:, span], preferred_element_type=F32)
        hidden = double_gelu(hidden * ROOT_HALF + b_ref[:, span] * ROOT_HALF)
        hidden_refs[s][i * piece : (i + 1) * piece] = hidden.astype(BF16).reshape(piece, rows, sub)

    def depth(s, c, total):
        span = slice(s * sub, (s + 1) * sub)
        near = [hidden_refs[s][c + k].reshape(rows // 16, 16, sub) for k in range(3)]
        sums = []
        for r in range(3):
            terms = [near[k] * tap_ref[3 * r + k, :, span][None] for k in range(3)]
            sums.append((terms[0] + terms[1] + terms[2]).reshape(rows, sub))
        summed = jnp.dot(shift, jnp.concatenate(sums, axis=0), preferred_element_type=F32)
        active = double_gelu(summed + db_ref[:, span] * ROOT_HALF)
        act_ref[c, :, span] = active.astype(BF16)
        return total + active.reshape(rows // 8, 8, sub).sum(0)

    for i in range(pieces):
        expand(0, i)
    for s in range(len(hidden_refs)):
        total = jnp.zeros((8, sub), F32)
        for i in range(pieces):
            if s + 1 < len(hidden_refs):
                expand(s + 1, i)
            for c in range(i * out_cols // pieces, (i + 1) * out_cols // pieces):
                total = depth(s, c, total)
        total_ref[:, s * sub : (s + 1) * sub] = total
    pooled = jnp.sum(total_ref[...], axis=0, keepdims=True)
    part = exact_dot(jnp.broadcast_to(pooled, (8, lanes)), down_ref[...])[None]

    @pl.when(pl.program_id(0) == 0)
    def _():
        part_ref[...] = jnp.broadcast_to(part, part_ref.shape)

    @pl.when(pl.program_id(0) > 0)
    def _():
        part_ref[...] += part


def row_shifts(rows):
    shift = np.zeros((rows, 3 * rows), np.float32)
    for offset in range(3):
        for row in range(rows):
            if 0 <= row + offset - 1 < rows:
                shift[row, offset * rows + row + offset - 1] = 1.0
    return jnp.asarray(shift, BF16)


def mbconv(
    count, field, before, after, expand_weight, expand_bias, depth_weight, depth_bias, squeeze_down
):
    cols, rows, channels = field.shape
    expanded = expand_weight.shape[1]
    squeeze = squeeze_down.shape[1]
    return pl.pallas_call(
        mbconv_kernel,
        name="mbconv",
        grid=(expanded // LANES,),
        in_specs=[
            whole(field.shape),
            whole(before.shape),
            whole(after.shape),
            pl.BlockSpec((channels, LANES), lambda i: (0, i)),
            pl.BlockSpec((1, LANES), lambda i: (0, i)),
            pl.BlockSpec((9, LANES), lambda i: (0, i)),
            pl.BlockSpec((1, LANES), lambda i: (0, i)),
            pl.BlockSpec((LANES, squeeze), lambda i: (i, 0)),
            pl.BlockSpec((rows, 3 * rows), lambda i: (0, 0)),
        ],
        out_specs=[
            pl.BlockSpec((cols, rows, LANES), lambda i: (0, 0, i)),
            pl.BlockSpec((count, 8, squeeze), lambda i: (0, 0, 0)),
        ],
        out_shape=[
            jax.ShapeDtypeStruct((cols, rows, expanded), BF16),
            jax.ShapeDtypeStruct((count, 8, squeeze), F32),
        ],
        scratch_shapes=[pltpu.VMEM((8, LANES), F32), pltpu.VMEM((9, 16, LANES), BF16)]
        + [pltpu.VMEM((cols + 2, rows, SUB), BF16)] * (LANES // SUB),
        cost_estimate=pl.CostEstimate(
            flops=2 * cols * rows * channels * expanded * 4,
            bytes_accessed=20_000_000,
            transcendentals=0,
        ),
        compiler_params=pltpu.CompilerParams(vmem_limit_bytes=VMEM_BYTES),
    )(
        field,
        before,
        after,
        expand_weight,
        expand_bias.reshape(1, -1),
        depth_weight,
        depth_bias.reshape(1, -1),
        squeeze_down,
        row_shifts(rows),
    )


def prepare(in_ref, wv_ref, mask_ref):
    channels = in_ref.shape[0]
    wv_ref[...] = in_ref[:, 2 * channels :].T
    head = lax.broadcasted_iota(jnp.int32, mask_ref.shape, 0) // CELLS
    lane = lax.broadcasted_iota(jnp.int32, mask_ref.shape, 1) // HEAD_DIM
    mask_ref[...] = (head == lane).astype(F32).astype(BF16)


def attend(stream, gain_ref, in_ref, out_weight_ref, bias_ref, scratch):
    wv_ref, mask_ref, q_ref, k_ref, vt_ref, o_ref = scratch
    cells, channels = stream.shape
    average = jnp.mean(stream, axis=-1, keepdims=True)
    centred = stream - average
    variance = jnp.mean(centred * centred, axis=-1, keepdims=True)
    normed = (centred * lax.rsqrt(variance + 1e-05) * gain_ref[...]).astype(BF16)
    q_ref[...] = jnp.dot(normed, in_ref[:, :channels], preferred_element_type=F32).astype(BF16)
    k_ref[...] = jnp.dot(
        normed, in_ref[:, channels : 2 * channels], preferred_element_type=F32
    ).astype(BF16)
    vt_ref[...] = lax.dot_general(
        wv_ref[...], normed, (((1,), (1,)), ((), ())), preferred_element_type=F32
    ).astype(BF16)
    group = 256 // HEAD_DIM
    even = (lax.broadcasted_iota(jnp.int32, (CELLS, 128), 1) // HEAD_DIM) % 2 == 0
    zero = jnp.zeros((CELLS, 128), BF16)
    for duo in range(cells // 128):
        both = slice(duo * 128, (duo + 1) * 128)
        for g in range(HEADS // group):
            part = slice(g * 256, (g + 1) * 256)
            lanes = slice(g * group * CELLS, (g + 1) * group * CELLS)
            probs = []
            for w in (2 * duo, 2 * duo + 1):
                span = slice(w * CELLS, (w + 1) * CELLS)
                query = jnp.concatenate([q_ref[span, part]] * group, axis=0) * mask_ref[...]
                scores = lax.dot_general(
                    k_ref[span, part], query, (((1,), (1,)), ((), ())), preferred_element_type=F32
                )
                scores = scores * SCORE_SCALE + bias_ref[:, lanes]
                scores = jnp.exp2(scores - jnp.max(scores, axis=0, keepdims=True))
                weight = 1.0 / jnp.sum(scores, axis=0, keepdims=True)
                probs.append((scores * weight).astype(BF16))
            for quad in range(group // 4):
                outs = []
                for pair in (2 * quad, 2 * quad + 1):
                    c = slice(pair * 128, (pair + 1) * 128)
                    right = jnp.concatenate(
                        [
                            jnp.concatenate([probs[0][:, c], zero], axis=1),
                            jnp.concatenate([zero, probs[1][:, c]], axis=1),
                        ],
                        axis=0,
                    )
                    first = g * 256 + pair * 64
                    outs.append(
                        jnp.dot(
                            vt_ref[first : first + 64, both], right, preferred_element_type=F32
                        )
                    )
                first = g * 256 + quad * 128
                for k in range(2):
                    turned = jnp.concatenate([o[:, k * 128 : (k + 1) * 128] for o in outs], axis=0)
                    turned = turned.T
                    picked = jnp.where(even, turned[:CELLS], turned[CELLS:])
                    row = (2 * duo + k) * CELLS
                    o_ref[row : row + CELLS, first : first + 128] = picked.astype(BF16)
    return stream + jnp.dot(o_ref[...], out_weight_ref[...], preferred_element_type=F32)


def block_kernel(
    scale, split, me_ref, act_ref, x_ref, part_ref, up_ref, proj_ref, gain_ref, in_ref,
    out_weight_ref, bias_ref, *refs,
):
    outs, (gate_ref, sent_ref, *scratch) = (refs[:WIN], refs[WIN:]) if split else (refs[:1], refs[1:])
    cols, rows, expanded = act_ref.shape
    channels = x_ref.shape[2]

    @pl.when(pl.program_id(0) == 0)
    def _():
        squeezed = jnp.sum(part_ref[...], axis=0) * scale
        squeezed = squeezed * jax.nn.sigmoid(squeezed)
        gate_ref[...] = jax.nn.sigmoid(exact_dot(squeezed, up_ref[...])) * ROOT_HALF
        prepare(in_ref, scratch[0], scratch[1])

    gated = act_ref[...].reshape(cols * rows, expanded).astype(F32) * gate_ref[0:1]
    first = jnp.dot(gated.astype(BF16), proj_ref[...], preferred_element_type=F32)
    first = first.reshape(cols, rows, channels) + x_ref[...].astype(F32)
    first = first.astype(BF16).astype(F32)
    windows = rows // WIN
    stream = jnp.concatenate(
        [first[:, a * WIN : (a + 1) * WIN].reshape(CELLS, channels) for a in range(windows)],
        axis=0,
    )
    second = attend(stream, gain_ref, in_ref, out_weight_ref, bias_ref, scratch)
    second = second.reshape(windows, cols, WIN, channels)
    second = jnp.concatenate([second[a] for a in range(windows)], axis=1).astype(BF16)
    deliver(second, me_ref, outs, sent_ref)


def deliver(pieces, me_ref, outs, sent_ref):
    if len(outs) == 1:
        outs[0][:, 0] = pieces
        return
    sent_ref[...] = pieces
    for s in range(WIN):
        outs[s][0] = sent_ref[me_ref[0] ^ s]


def gathered(ins):
    if len(ins) == 1:
        return ins[0][...].reshape(-1, ins[0].shape[-1])
    return jnp.concatenate([ref[0] for ref in ins], axis=0)


def grid_kernel(split_in, split_out, me_ref, *refs):
    n = WIN if split_in else 1
    ins, refs = refs[:n], refs[n:]
    perm_ref, gain_ref, in_ref, out_weight_ref, bias_ref = refs[:5]
    n = WIN if split_out else 1
    outs, (sent_ref, *scratch) = refs[5 : 5 + n], refs[5 + n :]

    @pl.when(pl.program_id(0) == 0)
    def _():
        prepare(in_ref, scratch[0], scratch[1])

    stream = jnp.dot(perm_ref[...], gathered(ins), preferred_element_type=F32)
    result = attend(stream, gain_ref, in_ref, out_weight_ref, bias_ref, scratch)
    channels = result.shape[1]
    result = result.reshape(-1, WIN, WIN, channels)
    result = jnp.concatenate([result[a] for a in range(result.shape[0])], axis=1).astype(BF16)
    deliver(result, me_ref, outs, sent_ref)


def merge_kernel(split, me_ref, *refs):
    n = WIN if split else 1
    ins, perm_ref, out_ref = refs[:n], refs[n], refs[-1]
    cells = jnp.dot(perm_ref[...], gathered(ins), preferred_element_type=F32)
    out_ref[...] = cells.reshape(out_ref.shape).astype(BF16)


def attention_scratch(cells, channels):
    return [
        pltpu.VMEM((channels, channels), BF16),
        pltpu.VMEM((256 // HEAD_DIM * CELLS, 256), BF16),
        pltpu.VMEM((cells, channels), BF16),
        pltpu.VMEM((cells, channels), BF16),
        pltpu.VMEM((channels, cells), BF16),
        pltpu.VMEM((cells, channels), BF16),
    ]


def partner_specs(split, rows, channels):
    if split:
        return [pl.BlockSpec((1, rows, channels), lambda b, me: (b, 0, 0))] * WIN
    return [pl.BlockSpec((WIN, 1, rows, channels), lambda b, me: (0, b, 0, 0))]


def partner_shapes(split, count, rows, channels):
    if split:
        return [jax.ShapeDtypeStruct((count, rows, channels), BF16)] * WIN
    return [jax.ShapeDtypeStruct((WIN, count, rows, channels), BF16)]


def block_stage(split, start, count, scale, me, active, field, parts, up, proj, params):
    cols, rows, channels = field.shape
    expanded = active.shape[2]
    cells = WIN * rows
    return pl.pallas_call(
        functools.partial(block_kernel, scale, split),
        name="block_stage",
        grid_spec=pltpu.PrefetchScalarGridSpec(
            num_scalar_prefetch=1,
            grid=(count,),
            in_specs=[
                pl.BlockSpec((WIN, rows, expanded), lambda b, me: (b + start, 0, 0)),
                pl.BlockSpec((WIN, rows, channels), lambda b, me: (b + start, 0, 0)),
            ]
            + [whole(p.shape) for p in (parts, up, proj, *params)],
            out_specs=partner_specs(split, rows, channels),
            scratch_shapes=[
                pltpu.VMEM((8, expanded), F32),
                pltpu.VMEM((WIN, rows, channels), BF16),
            ]
            + attention_scratch(cells, channels),
        ),
        out_shape=partner_shapes(split, count, rows, channels),
        cost_estimate=pl.CostEstimate(
            flops=1_000_000,
            bytes_accessed=100_000,
            transcendentals=0,
        ),
        compiler_params=pltpu.CompilerParams(vmem_limit_bytes=VMEM_BYTES),
    )(me, active, field, parts, up, proj, *params)


def grid_stage(split_in, split_out, me, received, perm, params):
    count, rows, channels = received[0].shape[-3:]
    cells = WIN * rows
    return pl.pallas_call(
        functools.partial(grid_kernel, split_in, split_out),
        name="grid_stage",
        grid_spec=pltpu.PrefetchScalarGridSpec(
            num_scalar_prefetch=1,
            grid=(count,),
            in_specs=partner_specs(split_in, rows, channels)
            + [whole((cells, cells))]
            + [whole(p.shape) for p in params],
            out_specs=partner_specs(split_out, rows, channels),
            scratch_shapes=[pltpu.VMEM((WIN, rows, channels), BF16)]
            + attention_scratch(cells, channels),
        ),
        out_shape=partner_shapes(split_out, count, rows, channels),
        cost_estimate=pl.CostEstimate(
            flops=1_000_000,
            bytes_accessed=100_000,
            transcendentals=0,
        ),
        compiler_params=pltpu.CompilerParams(vmem_limit_bytes=VMEM_BYTES),
    )(me, *received, perm, *params)


def merge_stage(split, start, total, me, received, perm, merged):
    count, rows, channels = received[0].shape[-3:]
    cells = WIN * rows
    n = len(received)
    return pl.pallas_call(
        functools.partial(merge_kernel, split),
        name="merge_stage",
        grid_spec=pltpu.PrefetchScalarGridSpec(
            num_scalar_prefetch=1,
            grid=(count,),
            in_specs=partner_specs(split, rows, channels)
            + [whole((cells, cells))]
            + [pl.BlockSpec(memory_space=pl.ANY)] * (merged is not None),
            out_specs=pl.BlockSpec((rows, WIN, channels), lambda b, me: (0, b + start, 0)),
        ),
        out_shape=jax.ShapeDtypeStruct((rows, total * WIN, channels), BF16),
        input_output_aliases={} if merged is None else {n + 2: 0},
        cost_estimate=pl.CostEstimate(
            flops=1_000_000,
            bytes_accessed=100_000,
            transcendentals=0,
        ),
        compiler_params=pltpu.CompilerParams(vmem_limit_bytes=VMEM_BYTES),
    )(me, *received, perm, *([] if merged is None else [merged]))


def turned_bias(pos_table):
    position = jnp.arange(CELLS)
    row = position % WIN
    col = position // WIN
    index = (row[None, :] - row[:, None] + 7) * 15 + (col[None, :] - col[:, None] + 7)
    one_hot = (index[:, :, None] == jnp.arange(225)[None, None, :]).astype(F32)
    bias = jnp.einsum("jir,rh->jhi", one_hot, pos_table * LOG2E, precision=lax.Precision.HIGHEST)
    return bias.reshape(CELLS, HEADS * CELLS)


def attention_params(gain, in_weight, out_weight, pos_table):
    return gain.reshape(1, -1), in_weight, out_weight, turned_bias(pos_table)


def cell_orders(rows, place):
    per = rows // WIN
    cells = jnp.arange(WIN * rows)
    window, col, row = cells // CELLS, cells // WIN % WIN, cells % WIN
    into = (col ^ place) * rows + row * per + window
    row, col = cells // WIN, cells % WIN
    back = (col ^ place) * rows + row % per * WIN + row // per
    return tuple((source[:, None] == cells[None, :]).astype(BF16) for source in (into, back))


def per_device(
    input_field,
    expand_weight,
    expand_bias,
    depth_weight,
    depth_bias,
    squeeze_down,
    squeeze_up,
    project_weight,
    block_gain,
    block_in_weight,
    block_out_weight,
    block_table,
    grid_gain,
    grid_in_weight,
    grid_out_weight,
    grid_table,
):
    rows, cols, channels = input_field.shape
    count = lax.axis_size("lon")
    per = count // WIN
    groups = [[j * per + r for j in range(WIN)] for r in range(per)]
    total = cols // WIN
    chunks = CHUNKS if sum(c[0] for c in CHUNKS) == total else ((total, False, False),)
    place = lax.axis_index("lon") // per
    places = {True: place.reshape(1).astype(jnp.int32), False: jnp.zeros((1,), jnp.int32)}
    edges = lax.optimization_barrier(input_field)
    before = lax.ppermute(
        jnp.swapaxes(edges[:, -1:], 0, 1),
        "lon",
        [(i, (i + 1) % count) for i in range(count)],
    )
    after = lax.ppermute(
        jnp.swapaxes(edges[:, :1], 0, 1),
        "lon",
        [((i + 1) % count, i) for i in range(count)],
    )
    field = jnp.swapaxes(input_field, 0, 1)
    active, part = mbconv(
        count, field, before, after, expand_weight, expand_bias, depth_weight, depth_bias,
        squeeze_down,
    )
    parts = lax.all_to_all(part, "lon", 0, 0, tiled=True)
    scale = ROOT_HALF / (rows * cols * count)
    into, back = {}, {}
    for split in sorted({split for _, *both in chunks for split in both}):
        into[split], back[split] = cell_orders(rows, places[split][0])
    block_params = attention_params(block_gain, block_in_weight, block_out_weight, block_table)
    grid_params = attention_params(grid_gain, grid_in_weight, grid_out_weight, grid_table)

    def exchange(split, pieces):
        if not split:
            return [
                lax.all_to_all(
                    pieces[0], "lon", 0, 0, axis_index_groups=groups, tiled=True
                )
            ]
        return [pieces[0]] + [
            lax.ppermute(
                pieces[s],
                "lon",
                [(j * per + r, (j ^ s) * per + r) for j in range(WIN) for r in range(per)],
            )
            for s in range(1, WIN)
        ]

    starts = [sum(c[0] for c in chunks[:k]) for k in range(len(chunks))]
    sent = [
        block_stage(
            split, start, size, scale, places[split], active, field, parts, squeeze_up,
            project_weight, block_params,
        )
        for start, (size, split, _) in zip(starts, chunks)
    ]
    if len(chunks) > 1:
        sent[1], grid_params, into, back = lax.optimization_barrier(
            (sent[1], grid_params, into, back)
        )
    received = [exchange(split, pieces) for pieces, (_, split, _) in zip(sent, chunks)]
    results = []
    for k, (_, split, returned) in enumerate(chunks):
        pieces = received[k]
        if k + 1 < len(chunks):
            pieces, _ = lax.optimization_barrier((pieces, sent[k + 1][0]))
        if k > 0 and chunks[k - 1][2]:
            pieces, _ = lax.optimization_barrier((pieces, results[k - 1][1:TIED]))
        me = places[split or returned]
        result = grid_stage(split, returned, me, pieces, into[split], grid_params)
        results.append(exchange(returned, result))
    merged = None
    for start, result, (_, _, split) in zip(starts, results, chunks):
        merged = merge_stage(
            split, start, total, places[split], result, back[split], merged
        )
    return merged


def solution(mesh):
    return jax.shard_map(
        per_device,
        mesh=mesh,
        in_specs=(P("groups", "lon", None),) + (P(),) * 15,
        out_specs=P("groups", "lon", None),
        check_vma=False,
    )
```

```python
import functools

import jax
import jax.numpy as jnp
import numpy as np
from jax import lax
from jax.experimental import pallas as pl
from jax.experimental.pallas import tpu as pltpu
from jax.sharding import PartitionSpec as P

HEADS = 16
HEAD_DIM = 32
WIN = 8
CELLS = WIN * WIN
CHUNKS = ((2, False, True), (2, False, True))
TIED = 4
LANES = 1024
SUB = 256
VMEM_BYTES = 60 << 20
ROOT_HALF = 0.7071067811865476
LOG2E = 1.4426950408889634
SCORE_SCALE = HEAD_DIM ** (-0.5) * LOG2E
BF16 = jnp.bfloat16
F32 = jnp.float32


def whole(shape):
    return pl.BlockSpec(shape, lambda *_: (0,) * len(shape), pipeline_mode=pl.Buffered(1))


def double_gelu(half):
    return half + half * lax.erf(half)


def exact_dot(values, weight):
    count = values.shape[0]
    high = values.astype(BF16).astype(F32)
    middle = (values - high).astype(BF16).astype(F32)
    parts = jnp.concatenate([high, middle, values - high - middle], axis=0).astype(BF16)
    sums = jnp.dot(parts, weight, preferred_element_type=F32)
    return sums[:count] + sums[count : 2 * count] + sums[2 * count :]


def mbconv_kernel(
    x_ref, before_ref, after_ref, w_ref, b_ref, dw_ref, db_ref, down_ref, shift_ref,
    act_ref, part_ref, total_ref, tap_ref, *hidden_refs,
):
    out_cols, rows, channels = x_ref.shape
    lanes = w_ref.shape[1]
    sub = hidden_refs[0].shape[2]
    half = out_cols // 2
    pieces = 2
    piece = half + 1
    shift = shift_ref[...]
    for k in range(9):
        tap_ref[k] = jnp.broadcast_to(dw_ref[k : k + 1] * 0.5, (16, lanes)).astype(BF16)

    def expand(s, i):
        span = slice(s * sub, (s + 1) * sub)
        if i == 0:
            cells = jnp.concatenate([before_ref[...], x_ref[:half]], axis=0)
        else:
            cells = jnp.concatenate([x_ref[half:], after_ref[...]], axis=0)
        cells = cells.reshape(piece * rows, channels)
        hidden = jnp.dot(cells, w_ref[:, span], preferred_element_type=F32)
        hidden = double_gelu(hidden * ROOT_HALF + b_ref[:, span] * ROOT_HALF)
        hidden_refs[s][i * piece : (i + 1) * piece] = hidden.astype(BF16).reshape(piece, rows, sub)

    def depth(s, c, total):
        span = slice(s * sub, (s + 1) * sub)
        near = [hidden_refs[s][c + k].reshape(rows // 16, 16, sub) for k in range(3)]
        sums = []
        for r in range(3):
            terms = [near[k] * tap_ref[3 * r + k, :, span][None] for k in range(3)]
            sums.append((terms[0] + terms[1] + terms[2]).reshape(rows, sub))
        summed = jnp.dot(shift, jnp.concatenate(sums, axis=0), preferred_element_type=F32)
        active = double_gelu(summed + db_ref[:, span] * ROOT_HALF)
        act_ref[c, :, span] = active.astype(BF16)
        return total + active.reshape(rows // 8, 8, sub).sum(0)

    for i in range(pieces):
        expand(0, i)
    for s in range(len(hidden_refs)):
        total = jnp.zeros((8, sub), F32)
        for i in range(pieces):
            if s + 1 < len(hidden_refs):
                expand(s + 1, i)
            for c in range(i * out_cols // pieces, (i + 1) * out_cols // pieces):
                total = depth(s, c, total)
        total_ref[:, s * sub : (s + 1) * sub] = total
    pooled = jnp.sum(total_ref[...], axis=0, keepdims=True)
    part = exact_dot(jnp.broadcast_to(pooled, (8, lanes)), down_ref[...])[None]

    @pl.when(pl.program_id(0) == 0)
    def _():
        part_ref[...] = jnp.broadcast_to(part, part_ref.shape)

    @pl.when(pl.program_id(0) > 0)
    def _():
        part_ref[...] += part


def row_shifts(rows):
    shift = np.zeros((rows, 3 * rows), np.float32)
    for offset in range(3):
        for row in range(rows):
            if 0 <= row + offset - 1 < rows:
                shift[row, offset * rows + row + offset - 1] = 1.0
    return jnp.asarray(shift, BF16)


def mbconv(
    count, field, before, after, expand_weight, expand_bias, depth_weight, depth_bias, squeeze_down
):
    cols, rows, channels = field.shape
    expanded = expand_weight.shape[1]
    squeeze = squeeze_down.shape[1]
    return pl.pallas_call(
        mbconv_kernel,
        name="mbconv",
        grid=(expanded // LANES,),
        in_specs=[
            whole(field.shape),
            whole(before.shape),
            whole(after.shape),
            pl.BlockSpec((channels, LANES), lambda i: (0, i)),
            pl.BlockSpec((1, LANES), lambda i: (0, i)),
            pl.BlockSpec((9, LANES), lambda i: (0, i)),
            pl.BlockSpec((1, LANES), lambda i: (0, i)),
            pl.BlockSpec((LANES, squeeze), lambda i: (i, 0)),
            pl.BlockSpec((rows, 3 * rows), lambda i: (0, 0)),
        ],
        out_specs=[
            pl.BlockSpec((cols, rows, LANES), lambda i: (0, 0, i)),
            pl.BlockSpec((count, 8, squeeze), lambda i: (0, 0, 0)),
        ],
        out_shape=[
            jax.ShapeDtypeStruct((cols, rows, expanded), BF16),
            jax.ShapeDtypeStruct((count, 8, squeeze), F32),
        ],
        scratch_shapes=[pltpu.VMEM((8, LANES), F32), pltpu.VMEM((9, 16, LANES), BF16)]
        + [pltpu.VMEM((cols + 2, rows, SUB), BF16)] * (LANES // SUB),
        cost_estimate=pl.CostEstimate(
            flops=2 * cols * rows * channels * expanded * 4,
            bytes_accessed=20_000_000,
            transcendentals=0,
        ),
        compiler_params=pltpu.CompilerParams(vmem_limit_bytes=VMEM_BYTES),
    )(
        field,
        before,
        after,
        expand_weight,
        expand_bias.reshape(1, -1),
        depth_weight,
        depth_bias.reshape(1, -1),
        squeeze_down,
        row_shifts(rows),
    )


def prepare(in_ref, wv_ref, mask_ref):
    channels = in_ref.shape[0]
    wv_ref[...] = in_ref[:, 2 * channels :].T
    head = lax.broadcasted_iota(jnp.int32, mask_ref.shape, 0) // CELLS
    lane = lax.broadcasted_iota(jnp.int32, mask_ref.shape, 1) // HEAD_DIM
    mask_ref[...] = (head == lane).astype(F32).astype(BF16)


def attend(stream, gain_ref, in_ref, out_weight_ref, bias_ref, scratch):
    wv_ref, mask_ref, q_ref, k_ref, vt_ref, o_ref = scratch
    cells, channels = stream.shape
    average = jnp.mean(stream, axis=-1, keepdims=True)
    centred = stream - average
    variance = jnp.mean(centred * centred, axis=-1, keepdims=True)
    normed = (centred * lax.rsqrt(variance + 1e-05) * gain_ref[...]).astype(BF16)
    q_ref[...] = jnp.dot(normed, in_ref[:, :channels], preferred_element_type=F32).astype(BF16)
    k_ref[...] = jnp.dot(
        normed, in_ref[:, channels : 2 * channels], preferred_element_type=F32
    ).astype(BF16)
    vt_ref[...] = lax.dot_general(
        wv_ref[...], normed, (((1,), (1,)), ((), ())), preferred_element_type=F32
    ).astype(BF16)
    group = 256 // HEAD_DIM
    even = (lax.broadcasted_iota(jnp.int32, (CELLS, 128), 1) // HEAD_DIM) % 2 == 0
    zero = jnp.zeros((CELLS, 128), BF16)
    for duo in range(cells // 128):
        both = slice(duo * 128, (duo + 1) * 128)
        for g in range(HEADS // group):
            part = slice(g * 256, (g + 1) * 256)
            lanes = slice(g * group * CELLS, (g + 1) * group * CELLS)
            probs = []
            for w in (2 * duo, 2 * duo + 1):
                span = slice(w * CELLS, (w + 1) * CELLS)
                query = jnp.concatenate([q_ref[span, part]] * group, axis=0) * mask_ref[...]
                scores = lax.dot_general(
                    k_ref[span, part], query, (((1,), (1,)), ((), ())), preferred_element_type=F32
                )
                scores = scores * SCORE_SCALE + bias_ref[:, lanes]
                scores = jnp.exp2(scores - jnp.max(scores, axis=0, keepdims=True))
                weight = 1.0 / jnp.sum(scores, axis=0, keepdims=True)
                probs.append((scores * weight).astype(BF16))
            for quad in range(group // 4):
                outs = []
                for pair in (2 * quad, 2 * quad + 1):
                    c = slice(pair * 128, (pair + 1) * 128)
                    right = jnp.concatenate(
                        [
                            jnp.concatenate([probs[0][:, c], zero], axis=1),
                            jnp.concatenate([zero, probs[1][:, c]], axis=1),
                        ],
                        axis=0,
                    )
                    first = g * 256 + pair * 64
                    outs.append(
                        jnp.dot(
                            vt_ref[first : first + 64, both], right, preferred_element_type=F32
                        )
                    )
                first = g * 256 + quad * 128
                for k in range(2):
                    turned = jnp.concatenate([o[:, k * 128 : (k + 1) * 128] for o in outs], axis=0)
                    turned = turned.T
                    picked = jnp.where(even, turned[:CELLS], turned[CELLS:])
                    row = (2 * duo + k) * CELLS
                    o_ref[row : row + CELLS, first : first + 128] = picked.astype(BF16)
    return stream + jnp.dot(o_ref[...], out_weight_ref[...], preferred_element_type=F32)


def block_kernel(
    scale, split, me_ref, act_ref, x_ref, part_ref, up_ref, proj_ref, gain_ref, in_ref,
    out_weight_ref, bias_ref, *refs,
):
    outs, (gate_ref, sent_ref, *scratch) = (refs[:WIN], refs[WIN:]) if split else (refs[:1], refs[1:])
    cols, rows, expanded = act_ref.shape
    channels = x_ref.shape[2]

    @pl.when(pl.program_id(0) == 0)
    def _():
        squeezed = jnp.sum(part_ref[...], axis=0) * scale
        squeezed = squeezed * jax.nn.sigmoid(squeezed)
        gate_ref[...] = jax.nn.sigmoid(exact_dot(squeezed, up_ref[...])) * ROOT_HALF
        prepare(in_ref, scratch[0], scratch[1])

    gated = act_ref[...].reshape(cols * rows, expanded).astype(F32) * gate_ref[0:1]
    first = jnp.dot(gated.astype(BF16), proj_ref[...], preferred_element_type=F32)
    first = first.reshape(cols, rows, channels) + x_ref[...].astype(F32)
    first = first.astype(BF16).astype(F32)
    windows = rows // WIN
    stream = jnp.concatenate(
        [first[:, a * WIN : (a + 1) * WIN].reshape(CELLS, channels) for a in range(windows)],
        axis=0,
    )
    second = attend(stream, gain_ref, in_ref, out_weight_ref, bias_ref, scratch)
    second = second.reshape(windows, cols, WIN, channels)
    second = jnp.concatenate([second[a] for a in range(windows)], axis=1).astype(BF16)
    deliver(second, me_ref, outs, sent_ref)


def deliver(pieces, me_ref, outs, sent_ref):
    if len(outs) == 1:
        outs[0][:, 0] = pieces
        return
    sent_ref[...] = pieces
    for s in range(WIN):
        outs[s][0] = sent_ref[me_ref[0] ^ s]


def gathered(ins):
    if len(ins) == 1:
        return ins[0][...].reshape(-1, ins[0].shape[-1])
    return jnp.concatenate([ref[0] for ref in ins], axis=0)


def grid_kernel(split_in, split_out, me_ref, *refs):
    n = WIN if split_in else 1
    ins, refs = refs[:n], refs[n:]
    perm_ref, gain_ref, in_ref, out_weight_ref, bias_ref = refs[:5]
    n = WIN if split_out else 1
    outs, (sent_ref, *scratch) = refs[5 : 5 + n], refs[5 + n :]

    @pl.when(pl.program_id(0) == 0)
    def _():
        prepare(in_ref, scratch[0], scratch[1])

    stream = jnp.dot(perm_ref[...], gathered(ins), preferred_element_type=F32)
    result = attend(stream, gain_ref, in_ref, out_weight_ref, bias_ref, scratch)
    channels = result.shape[1]
    result = result.reshape(-1, WIN, WIN, channels)
    result = jnp.concatenate([result[a] for a in range(result.shape[0])], axis=1).astype(BF16)
    deliver(result, me_ref, outs, sent_ref)


def merge_kernel(split, me_ref, *refs):
    n = WIN if split else 1
    ins, perm_ref, out_ref = refs[:n], refs[n], refs[-1]
    cells = jnp.dot(perm_ref[...], gathered(ins), preferred_element_type=F32)
    out_ref[...] = cells.reshape(out_ref.shape).astype(BF16)


def attention_scratch(cells, channels):
    return [
        pltpu.VMEM((channels, channels), BF16),
        pltpu.VMEM((256 // HEAD_DIM * CELLS, 256), BF16),
        pltpu.VMEM((cells, channels), BF16),
        pltpu.VMEM((cells, channels), BF16),
        pltpu.VMEM((channels, cells), BF16),
        pltpu.VMEM((cells, channels), BF16),
    ]


def partner_specs(split, rows, channels):
    if split:
        return [pl.BlockSpec((1, rows, channels), lambda b, me: (b, 0, 0))] * WIN
    return [pl.BlockSpec((WIN, 1, rows, channels), lambda b, me: (0, b, 0, 0))]


def partner_shapes(split, count, rows, channels):
    if split:
        return [jax.ShapeDtypeStruct((count, rows, channels), BF16)] * WIN
    return [jax.ShapeDtypeStruct((WIN, count, rows, channels), BF16)]


def block_stage(split, start, count, scale, me, active, field, parts, up, proj, params):
    cols, rows, channels = field.shape
    expanded = active.shape[2]
    cells = WIN * rows
    return pl.pallas_call(
        functools.partial(block_kernel, scale, split),
        name="block_stage",
        grid_spec=pltpu.PrefetchScalarGridSpec(
            num_scalar_prefetch=1,
            grid=(count,),
            in_specs=[
                pl.BlockSpec((WIN, rows, expanded), lambda b, me: (b + start, 0, 0)),
                pl.BlockSpec((WIN, rows, channels), lambda b, me: (b + start, 0, 0)),
            ]
            + [whole(p.shape) for p in (parts, up, proj, *params)],
            out_specs=partner_specs(split, rows, channels),
            scratch_shapes=[
                pltpu.VMEM((8, expanded), F32),
                pltpu.VMEM((WIN, rows, channels), BF16),
            ]
            + attention_scratch(cells, channels),
        ),
        out_shape=partner_shapes(split, count, rows, channels),
        cost_estimate=pl.CostEstimate(
            flops=1_000_000,
            bytes_accessed=100_000,
            transcendentals=0,
        ),
        compiler_params=pltpu.CompilerParams(vmem_limit_bytes=VMEM_BYTES),
    )(me, active, field, parts, up, proj, *params)


def grid_stage(split_in, split_out, me, received, perm, params):
    count, rows, channels = received[0].shape[-3:]
    cells = WIN * rows
    return pl.pallas_call(
        functools.partial(grid_kernel, split_in, split_out),
        name="grid_stage",
        grid_spec=pltpu.PrefetchScalarGridSpec(
            num_scalar_prefetch=1,
            grid=(count,),
            in_specs=partner_specs(split_in, rows, channels)
            + [whole((cells, cells))]
            + [whole(p.shape) for p in params],
            out_specs=partner_specs(split_out, rows, channels),
            scratch_shapes=[pltpu.VMEM((WIN, rows, channels), BF16)]
            + attention_scratch(cells, channels),
        ),
        out_shape=partner_shapes(split_out, count, rows, channels),
        cost_estimate=pl.CostEstimate(
            flops=1_000_000,
            bytes_accessed=100_000,
            transcendentals=0,
        ),
        compiler_params=pltpu.CompilerParams(vmem_limit_bytes=VMEM_BYTES),
    )(me, *received, perm, *params)


def merge_stage(split, start, total, me, received, perm, merged):
    count, rows, channels = received[0].shape[-3:]
    cells = WIN * rows
    n = len(received)
    return pl.pallas_call(
        functools.partial(merge_kernel, split),
        name="merge_stage",
        grid_spec=pltpu.PrefetchScalarGridSpec(
            num_scalar_prefetch=1,
            grid=(count,),
            in_specs=partner_specs(split, rows, channels)
            + [whole((cells, cells))]
            + [pl.BlockSpec(memory_space=pl.ANY)] * (merged is not None),
            out_specs=pl.BlockSpec((rows, WIN, channels), lambda b, me: (0, b + start, 0)),
        ),
        out_shape=jax.ShapeDtypeStruct((rows, total * WIN, channels), BF16),
        input_output_aliases={} if merged is None else {n + 2: 0},
        cost_estimate=pl.CostEstimate(
            flops=1_000_000,
            bytes_accessed=100_000,
            transcendentals=0,
        ),
        compiler_params=pltpu.CompilerParams(vmem_limit_bytes=VMEM_BYTES),
    )(me, *received, perm, *([] if merged is None else [merged]))


def turned_bias(pos_table):
    position = jnp.arange(CELLS)
    row = position % WIN
    col = position // WIN
    index = (row[None, :] - row[:, None] + 7) * 15 + (col[None, :] - col[:, None] + 7)
    one_hot = (index[:, :, None] == jnp.arange(225)[None, None, :]).astype(F32)
    bias = jnp.einsum("jir,rh->jhi", one_hot, pos_table * LOG2E, precision=lax.Precision.HIGHEST)
    return bias.reshape(CELLS, HEADS * CELLS)


def attention_params(gain, in_weight, out_weight, pos_table):
    return gain.reshape(1, -1), in_weight, out_weight, turned_bias(pos_table)


def cell_orders(rows, place):
    per = rows // WIN
    cells = jnp.arange(WIN * rows)
    window, col, row = cells // CELLS, cells // WIN % WIN, cells % WIN
    into = (col ^ place) * rows + row * per + window
    row, col = cells // WIN, cells % WIN
    back = (col ^ place) * rows + row % per * WIN + row // per
    return tuple((source[:, None] == cells[None, :]).astype(BF16) for source in (into, back))


def per_device(
    input_field,
    expand_weight,
    expand_bias,
    depth_weight,
    depth_bias,
    squeeze_down,
    squeeze_up,
    project_weight,
    block_gain,
    block_in_weight,
    block_out_weight,
    block_table,
    grid_gain,
    grid_in_weight,
    grid_out_weight,
    grid_table,
):
    rows, cols, channels = input_field.shape
    count = lax.axis_size("lon")
    per = count // WIN
    groups = [[j * per + r for j in range(WIN)] for r in range(per)]
    total = cols // WIN
    chunks = CHUNKS if sum(c[0] for c in CHUNKS) == total else ((total, False, False),)
    place = lax.axis_index("lon") // per
    places = {True: place.reshape(1).astype(jnp.int32), False: jnp.zeros((1,), jnp.int32)}
    edges = lax.optimization_barrier(input_field)
    before = lax.ppermute(
        jnp.swapaxes(edges[:, -1:], 0, 1),
        "lon",
        [(i, (i + 1) % count) for i in range(count)],
    )
    after = lax.ppermute(
        jnp.swapaxes(edges[:, :1], 0, 1),
        "lon",
        [((i + 1) % count, i) for i in range(count)],
    )
    field = jnp.swapaxes(input_field, 0, 1)
    active, part = mbconv(
        count, field, before, after, expand_weight, expand_bias, depth_weight, depth_bias,
        squeeze_down,
    )
    parts = lax.all_to_all(part, "lon", 0, 0, tiled=True)
    scale = ROOT_HALF / (rows * cols * count)
    into, back = {}, {}
    for split in sorted({split for _, *both in chunks for split in both}):
        into[split], back[split] = cell_orders(rows, places[split][0])
    block_params = attention_params(block_gain, block_in_weight, block_out_weight, block_table)
    grid_params = attention_params(grid_gain, grid_in_weight, grid_out_weight, grid_table)

    def exchange(split, pieces):
        if not split:
            return [
                lax.all_to_all(
                    pieces[0], "lon", 0, 0, axis_index_groups=groups, tiled=True
                )
            ]
        return [pieces[0]] + [
            lax.ppermute(
                pieces[s],
                "lon",
                [(j * per + r, (j ^ s) * per + r) for j in range(WIN) for r in range(per)],
            )
            for s in range(1, WIN)
        ]

    starts = [sum(c[0] for c in chunks[:k]) for k in range(len(chunks))]
    sent = [
        block_stage(
            split, start, size, scale, places[split], active, field, parts, squeeze_up,
            project_weight, block_params,
        )
        for start, (size, split, _) in zip(starts, chunks)
    ]
    if len(chunks) > 1:
        sent[1], grid_params, into, back = lax.optimization_barrier(
            (sent[1], grid_params, into, back)
        )
    received = [exchange(split, pieces) for pieces, (_, split, _) in zip(sent, chunks)]
    results = []
    for k, (_, split, returned) in enumerate(chunks):
        pieces = received[k]
        if k + 1 < len(chunks):
            pieces, _ = lax.optimization_barrier((pieces, sent[k + 1][0]))
        if k > 0 and chunks[k - 1][2]:
            pieces, _ = lax.optimization_barrier((pieces, results[k - 1][1:TIED]))
        me = places[split or returned]
        result = grid_stage(split, returned, me, pieces, into[split], grid_params)
        results.append(exchange(returned, result))
    merged = None
    for start, result, (_, _, split) in zip(starts, results, chunks):
        merged = merge_stage(
            split, start, total, places[split], result, back[split], merged
        )
    return merged


def solution(mesh):
    return jax.shard_map(
        per_device,
        mesh=mesh,
        in_specs=(P("groups", "lon", None),) + (P(),) * 15,
        out_specs=P("groups", "lon", None),
        check_vma=False,
    )
```
